512 devices in a mesh: blk: 32 (over y, z_lo), shard: 16 (over x, z_hi, core).
Axes of the slice: x: 4, y: 4, z: 16 (z_hi: 2, z_lo: 8; z = z_hi * 8 + z_lo), core: 2. Of those that a mesh axis runs over, the one named last changes fastest.
Arguments:
- weights: bfloat16 [32, 8192, 2048], P('blk', 'shard'), may hold values from -90 to 90
- warm_factor: float32 [32, 32, 2048], P('blk'), may hold values from -6 to 6
Outputs:
- new_weights: bfloat16 [32, 8192, 2048], P('blk', 'shard')
- new_factor: float32 [32, 32, 2048], P('blk', None, 'shard')
The draws below stay inside these ranges and needn't reach their ends.
All inputs are finite; a program needn't handle non-finite values.
Results may differ from the reference program's by a relative error of at most 0.012.
Values may be sent and summed in bfloat16 or wider, within the bound.
A program may use at most 64 MiB of HBM per device.

```python
from functools import partial
import jax
import jax.numpy as jnp
from jax import lax

HID = 8192
WID = 2048
RANK = 32
POWER = 4
REPLICAS = 32


def draw_weights(key, part):
    components = 3 * RANK // 2
    falloff = jnp.exp(jnp.log(0.25) / (RANK // 2) * jnp.arange(components, dtype=jnp.float32))
    row_place = jnp.arange(HID, dtype=jnp.float32) / HID
    roughness = jnp.exp(jax.random.uniform(jax.random.fold_in(key, 11), (HID,), minval=0.0, maxval=jnp.log(10.0)))
    row_scale = jnp.exp(jnp.log(3.0) * row_place) * roughness / 4.0
    left_vectors = jax.random.truncated_normal(jax.random.fold_in(key, 21), -3.0, 3.0, (REPLICAS, components, HID))
    right_vectors = jax.random.truncated_normal(jax.random.fold_in(key, 22), -3.0, 3.0, (REPLICAS, components, WID))
    amplitude = 0.44
    common_part = jnp.zeros((1, HID, WID), jnp.float32)
    noise = 0.25 * jax.random.truncated_normal(jax.random.fold_in(key, 13), -4.0, 4.0, (REPLICAS, HID, WID))
    weighted = left_vectors * (amplitude * falloff)[None, :, None]
    structured = jnp.einsum('rkh,rkw->rhw', weighted, right_vectors)
    values = (common_part + structured + noise) * row_scale[None, :, None]
    return jnp.clip(values, -90.0, 90.0).astype(jnp.bfloat16)


def shard_levels(own_key, shape, cuts, low, largest):
    factor_of = 1.0
    for dim, parts in cuts:
        draws = jax.random.uniform(jax.random.fold_in(jax.random.fold_in(own_key, 6), dim), (parts,), jnp.float32, low / len(cuts), largest / len(cuts))
        factor_of = factor_of * jnp.repeat(jnp.exp(draws), shape[dim] // parts).reshape((-1,) + (1,) * (len(shape) - 1 - dim))
    return factor_of


def gaussian(own_key, dims, width, limit, pieces=(), kind=jnp.bfloat16):
    loudness = shard_levels(own_key, dims, pieces, -0.22, 0.18) if pieces else 1.0
    entries = jax.random.normal(own_key, dims, jnp.float32) * width * loudness
    return jnp.minimum(jnp.maximum(entries, -limit), limit).astype(kind)


def setup_inputs(seed: int = 0) -> dict:
    arg_keys = jax.random.split(jax.random.key(seed), 3)
    weights = draw_weights(jax.random.fold_in(arg_keys[2], 71), 0)
    warm_factor = gaussian(arg_keys[1], (REPLICAS, RANK, WID), 1.0, 6.0, ((0, 32),), jnp.float32)
    return dict(weights=weights, warm_factor=warm_factor)


MIXING = 1.0 / 3.0

def power_edge(weights, arguments):
    edge_index, factor = arguments
    following = jnp.remainder(edge_index + 1, REPLICAS).astype(jnp.int32)
    lower_weight = lax.dynamic_index_in_dim(weights, edge_index.astype(jnp.int32), 0, keepdims=False)
    upper_weight = lax.dynamic_index_in_dim(weights, following, 0, keepdims=False)
    difference = lower_weight.astype(jnp.float32) - upper_weight.astype(jnp.float32)
    basis_rounded = jnp.zeros((RANK, HID), jnp.bfloat16)
    for iteration in range(POWER):
        rounded = lax.optimization_barrier(factor.astype(jnp.bfloat16))
        raw_factor = jnp.dot(rounded.astype(jnp.float32), difference.T, precision=lax.Precision.HIGHEST)
        gram = jnp.dot(raw_factor, raw_factor.T, precision=lax.Precision.HIGHEST)
        lower_factor = jnp.linalg.cholesky(gram)
        basis = jax.scipy.linalg.solve_triangular(lower_factor, raw_factor, lower=True)
        basis_rounded = lax.optimization_barrier(basis.astype(jnp.bfloat16))
        factor = jnp.dot(basis_rounded.astype(jnp.float32), difference, precision=lax.Precision.HIGHEST)
    return (basis_rounded, factor)

def reference(weights, warm_factor):
    edges = jnp.arange(REPLICAS, dtype=jnp.int32)
    bases, factors = lax.map(partial(power_edge, weights), (edges, warm_factor))
    final_rounded = factors.astype(jnp.bfloat16)

    def update(replica):
        prior = jnp.remainder(replica - 1 + REPLICAS, REPLICAS).astype(jnp.int32)
        replica = replica.astype(jnp.int32)
        signed = jnp.concatenate([lax.dynamic_index_in_dim(bases, prior, 0, keepdims=False), -lax.dynamic_index_in_dim(bases, replica, 0, keepdims=False)], axis=0)
        factor_pair = jnp.concatenate([lax.dynamic_index_in_dim(final_rounded, prior, 0, keepdims=False), lax.dynamic_index_in_dim(final_rounded, replica, 0, keepdims=False)], axis=0)
        delta = jnp.dot(signed.T.astype(jnp.float32), factor_pair.astype(jnp.float32), preferred_element_type=jnp.float32)
        own_weight = lax.dynamic_index_in_dim(weights, replica, 0, keepdims=False)
        return (own_weight.astype(jnp.float32) + MIXING * delta).astype(jnp.bfloat16)
    new_weights = lax.map(update, edges)
    return (new_weights, factors)
```

```python
import jax
import jax.numpy as jnp
from jax import lax
from jax.experimental import pallas as pl
from jax.experimental.pallas import tpu as pltpu
from jax.sharding import PartitionSpec as P

POWER = 4
MIXING = 1.0 / 3.0
MESH = pl.DeviceIdType.MESH
HIGHEST = lax.Precision.HIGHEST
F32 = jnp.float32
BF16 = jnp.bfloat16

RANK = 32
RING = 8
ROWS = 512
WID = 2048
LANES = 128
CHUNKS = 4
CHUNK_ROWS = ROWS // CHUNKS


def mix(a, b, dims):
    return lax.dot_general(a, b, (dims, ((), ())), preferred_element_type=F32)


def mix_exact(a, b, dims):
    return lax.dot_general(
        a, b, (dims, ((), ())), precision=HIGHEST, preferred_element_type=F32
    )


def inverse_lower(packed):
    lane = lax.broadcasted_iota(jnp.int32, (8, LANES), 1)
    row = lax.broadcasted_iota(jnp.int32, (8, LANES), 0)
    parts = []
    for j in range(4):
        shift = (RANK - RANK * j) % LANES
        moved = packed if shift == 0 else pltpu.roll(packed, shift, 1)
        unit = (lane == row + 8 * j).astype(F32)
        parts.append(jnp.where(lane < RANK, unit, jnp.where(lane < 2 * RANK, moved, 0.0)))
    for k in range(RANK):
        own = k // 8
        pivot_row = parts[own][k % 8 : k % 8 + 1, :]
        columns = {}
        for i in range(own, 4):
            columns[i] = jnp.broadcast_to(parts[i][:, RANK + k : RANK + k + 1], (8, LANES))
        pivot = columns[own][k % 8 : k % 8 + 1, :]
        scaled = pivot_row / pivot
        for i in range(own, 4):
            column = columns[i]
            if i == own:
                column = jnp.where(row > k % 8, column, 0.0)
            parts[i] = parts[i] - column * scaled
    done = []
    for j in range(4):
        diagonal = jnp.sum(
            jnp.where(lane == row + RANK + 8 * j, parts[j], 0.0), axis=1, keepdims=True
        )
        done.append(jnp.where(lane < RANK, parts[j] / jnp.sqrt(diagonal), 0.0))
    return jnp.concatenate(done, axis=0)


def kernel(
    w_hbm,
    warm_ref,
    signed_ref,
    pair_ref,
    new_ref,
    wbuf,
    wside,
    fbuf,
    fprior,
    bprior,
    raw,
    halves,
    partial,
    arrived,
    gram_own,
    gram_all,
    gram_plane,
    gram_far,
    plane,
    far,
    summed,
    basis,
    w_sem,
    ws_sem,
    wr_sem,
    gs_sem,
    gr_sem,
    ps_sem,
    pr_sem,
    zs_sem,
    zr_sem,
    zgs_sem,
    zgr_sem,
    fs_sem,
    fr_sem,
    es_sem,
    er_sem,
    bs_sem,
    br_sem,
    hs_sem,
    hr_sem,
):
    blk = lax.axis_index("blk")
    shard = lax.axis_index("shard")
    blks = lax.axis_size("blk")
    x = shard // 4
    far_half = lax.rem(shard // 2, 2)
    core = lax.rem(shard, 2)
    place = 2 * x + core
    above = lax.rem(blk + 1, blks)
    below = lax.rem(blk + blks - 1, blks)
    across = 4 * x + 2 * (1 - far_half) + core
    turns_up = lax.rem(blk, RING) // (RING - 1)
    turns_down = (RING - 1 - lax.rem(blk, RING)) // (RING - 1)
    half_up = lax.rem(far_half + turns_up, 2)
    half_down = lax.rem(far_half + turns_down, 2)
    shard_up = 4 * x + 2 * half_up + core
    shard_down = 4 * x + 2 * half_down + core

    def mate(dx, dc):
        return 4 * lax.rem(x + dx, 4) + 2 * far_half + lax.rem(core + dc, 2)


    others = [(dx, dc) for dx in (2, 1, 3, 0) for dc in (0, 1) if dx or dc]

    def remote(src, dst, send, recv, to_blk, to_shard):
        return pltpu.make_async_remote_copy(
            src_ref=src,
            dst_ref=dst,
            send_sem=send,
            recv_sem=recv,
            device_id=(to_blk, to_shard),
            device_id_type=MESH,
        )

    barrier = pltpu.get_barrier_semaphore()
    greeted = [(below, shard), (above, shard), (blk, across), (above, shard_up), (below, shard_down)]
    greeted += [(blk, mate(dx, dc)) for dx, dc in others]
    for peer in greeted:
        pl.semaphore_signal(barrier, inc=1, device_id=peer, device_id_type=MESH)
    load = pltpu.make_async_copy(w_hbm, wbuf.at[pl.ds(0, ROWS), :], w_sem)
    load.start()
    for q in range(16):
        fbuf[q] = warm_ref[:, q * LANES : (q + 1) * LANES].astype(BF16)
    raw[...] = jnp.zeros_like(raw)
    summed[...] = jnp.zeros_like(summed)
    pl.semaphore_wait(barrier, len(greeted))

    def weight_copy(c):
        rows = pl.ds(c * CHUNK_ROWS, CHUNK_ROWS)
        return remote(
            w_hbm.at[rows, :],
            wbuf.at[pl.ds(ROWS + c * CHUNK_ROWS, CHUNK_ROWS), :],
            ws_sem.at[c],
            wr_sem.at[c],
            below,
            shard,
        )

    for c in range(CHUNKS):
        weight_copy(c).start()
    load.wait()

    def turn(c):
        start = c * CHUNK_ROWS
        for q in range(16):
            wside[q * LANES : (q + 1) * LANES, start : start + CHUNK_ROWS] = wbuf[
                start : start + CHUNK_ROWS, q * LANES : (q + 1) * LANES
            ].T

    for c in range(CHUNKS):
        turn(c)
    for c in range(CHUNKS):
        weight_copy(c).wait_recv()
        turn(CHUNKS + c)
    for c in range(CHUNKS):
        weight_copy(c).wait_send()

    lane8 = lax.broadcasted_iota(jnp.int32, (8, LANES), 1) // RANK

    def gram_copy(dx, dc):
        t = 2 * dx + dc
        return remote(
            gram_own, gram_all.at[place], gs_sem.at[t], gr_sem.at[t], blk, mate(dx, dc)
        )

    def part_copy(j, dx, dc):
        t = 2 * dx + dc
        return remote(
            partial.at[j, t], arrived.at[j, t], ps_sem.at[j, t], pr_sem.at[j, t], blk, mate(dx, dc)
        )

    def gather_copy(j, dx, dc):
        t = 2 * dx + dc
        q = 4 * x + 2 * j + core
        return remote(
            fbuf.at[q], fbuf.at[q], fs_sem.at[j, t], fr_sem.at[j, t], blk, mate(dx, dc)
        )

    def far_gram_copy(slot):
        return remote(gram_plane.at[slot], gram_far.at[slot], zgs_sem.at[slot], zgr_sem.at[slot], blk, across)

    def far_copy(slot, j):
        return remote(plane.at[slot, j], far.at[slot, j], zs_sem.at[slot, j], zr_sem.at[slot, j], blk, across)

    def up_copy(j):
        q = 4 * x + 2 * j + core
        return remote(fbuf.at[q], fprior.at[q], es_sem.at[j], er_sem.at[j], above, shard_up)

    def pass_copy(j, dx, dc):
        t = 2 * dx + dc
        q = 4 * x + 2 * j + core
        return remote(
            fprior.at[q], fprior.at[q], hs_sem.at[j, t], hr_sem.at[j, t], blk, mate(dx, dc)
        )

    basis_copy = remote(basis, bprior, bs_sem, br_sem, above, shard)

    def step(k, carry):
        slot = lax.rem(k, 2)
        factor = jnp.concatenate([fbuf[q] for q in range(16)], axis=1)
        own = mix(factor, wside[...], ((1,), (0,)))
        raw_now = own[:, :ROWS] - own[:, ROWS:]
        raw[0:RANK, :] = raw_now
        stacked = jnp.concatenate([raw_now] * 4, axis=0)
        gram4 = mix_exact(raw_now, stacked, ((1,), (1,)))
        packed = gram4[0:8]
        for j in range(1, 4):
            packed = jnp.where(lane8 == j, gram4[8 * j : 8 * j + 8], packed)
        gram_own[...] = packed
        gram_all[place] = packed
        for dx, dc in others:
            gram_copy(dx, dc).start()
        high = raw_now.astype(BF16)
        low = (raw_now - high.astype(F32)).astype(BF16)
        halves[0:RANK, :ROWS] = high
        halves[0:RANK, ROWS:] = -high
        halves[RANK:, :ROWS] = low
        halves[RANK:, ROWS:] = -low

        for j in range(2):
            for dx in (2, 1, 3, 0):
                start = pl.multiple_of(512 * lax.rem(x + dx, 4) + 256 * j, 256)
                both = mix(halves[...], wbuf[:, pl.ds(start, 256)], ((1,), (0,)))
                piece = both[:RANK] + both[RANK:]
                first = 2 * dx + core
                second = 2 * dx + 1 - core
                if dx:
                    partial[j, first] = piece[:, :LANES]
                    partial[j, second] = piece[:, LANES:]
                    part_copy(j, dx, 0).start()
                    part_copy(j, dx, 1).start()
                else:
                    partial[j, first] = piece[:, :LANES]
                    partial[j, second] = piece[:, LANES:]
                    part_copy(j, 0, 1).start()
            if j == 0:
                for dx, dc in others:
                    gram_copy(dx, dc).wait_recv()
                gram_plane[slot] = jnp.sum(gram_all[...], axis=0)
                far_gram_copy(slot).start()
        for j in range(2):
            total = partial[j, 0]
            for dx, dc in others:
                part_copy(j, dx, dc).wait_recv()
            for t in range(1, 8):
                total = total + arrived[j, t]
            plane[slot, j] = total
            far_copy(slot, j).start()
        far_gram_copy(slot).wait_recv()
        lower_inv = inverse_lower(gram_plane[slot] + gram_far[slot])

        @pl.when(k == POWER - 1)
        def _():
            basis[...] = mix_exact(lower_inv, raw[...], ((1,), (0,))).astype(BF16)
            basis_copy.start()

        for dx, dc in others:
            for j in range(2):
                part_copy(j, dx, dc).wait_send()
        for j in range(2):
            far_copy(slot, j).wait_recv()
            summed[0:RANK, :] = plane[slot, j] + far[slot, j]
            piece = mix_exact(lower_inv, summed[...], ((1,), (0,)))
            fbuf[4 * x + 2 * j + core] = piece.astype(BF16)

            @pl.when(k == POWER - 1)
            def _():
                @pl.when(far_half == j)
                def _():
                    new_ref[...] = piece

                up_copy(j).start()

            for dx, dc in others:
                gather_copy(j, dx, dc).start()
        for dx, dc in others:
            gram_copy(dx, dc).wait_send()
        far_gram_copy(slot).wait_send()
        for j in range(2):
            far_copy(slot, j).wait_send()
        for j in range(2):
            for dx, dc in others:
                gather_copy(j, dx, dc).wait()
        return carry

    lax.fori_loop(0, POWER, step, 0)

    for j in range(2):
        up_copy(j).wait_recv()
        for dx, dc in others:
            pass_copy(j, dx, dc).start()
    for q in range(16):
        pair_ref[RANK:, q * LANES : (q + 1) * LANES] = fbuf[q]
    signed_ref[RANK:, :] = -basis[...]
    basis_copy.wait_recv()
    signed_ref[0:RANK, :] = bprior[...]
    for j in range(2):
        for dx, dc in others:
            pass_copy(j, dx, dc).wait()
    for q in range(16):
        pair_ref[0:RANK, q * LANES : (q + 1) * LANES] = fprior[q]
    basis_copy.wait_send()
    for j in range(2):
        up_copy(j).wait_send()


def on_device(weights, warm_factor):
    local_weight = weights[0]
    vmem = pl.BlockSpec(memory_space=pltpu.VMEM)
    dma = pltpu.SemaphoreType.DMA
    signed, factor_pair, new_factor = pl.pallas_call(
        kernel,
        out_shape=(
            jax.ShapeDtypeStruct((2 * RANK, ROWS), BF16),
            jax.ShapeDtypeStruct((2 * RANK, WID), BF16),
            jax.ShapeDtypeStruct((RANK, LANES), F32),
        ),
        in_specs=[pl.BlockSpec(memory_space=pl.ANY), vmem],
        out_specs=(vmem, vmem, vmem),
        scratch_shapes=[
            pltpu.VMEM((2 * ROWS, WID), BF16),
            pltpu.VMEM((WID, 2 * ROWS), BF16),
            pltpu.VMEM((16, RANK, LANES), BF16),
            pltpu.VMEM((16, RANK, LANES), BF16),
            pltpu.VMEM((RANK, ROWS), BF16),
            pltpu.VMEM((LANES, ROWS), F32),
            pltpu.VMEM((2 * RANK, 2 * ROWS), BF16),
            pltpu.VMEM((2, 8, RANK, LANES), F32),
            pltpu.VMEM((2, 8, RANK, LANES), F32),
            pltpu.VMEM((8, LANES), F32),
            pltpu.VMEM((8, 8, LANES), F32),
            pltpu.VMEM((2, 8, LANES), F32),
            pltpu.VMEM((2, 8, LANES), F32),
            pltpu.VMEM((2, 2, RANK, LANES), F32),
            pltpu.VMEM((2, 2, RANK, LANES), F32),
            pltpu.VMEM((LANES, LANES), F32),
            pltpu.VMEM((RANK, ROWS), BF16),
            dma,
            dma((CHUNKS,)),
            dma((CHUNKS,)),
            dma((8,)),
            dma((8,)),
            dma((2, 8)),
            dma((2, 8)),
            dma((2, 2)),
            dma((2, 2)),
            dma((2,)),
            dma((2,)),
            dma((2, 8)),
            dma((2, 8)),
            dma((2,)),
            dma((2,)),
            dma,
            dma,
            dma((2, 8)),
            dma((2, 8)),
        ],
        compiler_params=pltpu.CompilerParams(collective_id=0, has_side_effects=True),
        name="power_rounds",
    )(local_weight, warm_factor[0])
    delta = jnp.einsum("jr,jc->rc", signed, factor_pair, preferred_element_type=F32)
    new_weight = (local_weight.astype(F32) + MIXING * delta).astype(BF16)
    return (new_weight[None], new_factor[None])


def solution(mesh):
    return jax.shard_map(
        on_device,
        mesh=mesh,
        in_specs=(P("blk", "shard", None), P("blk", None, None)),
        out_specs=(P("blk", "shard", None), P("blk", None, "shard")),
        check_vma=False,
    )
```

```python
import jax
import jax.numpy as jnp
from jax import lax
from jax.experimental import pallas as pl
from jax.experimental.pallas import tpu as pltpu
from jax.sharding import PartitionSpec as P

POWER = 4
MIXING = 1.0 / 3.0
MESH = pl.DeviceIdType.MESH
HIGHEST = lax.Precision.HIGHEST
F32 = jnp.float32
BF16 = jnp.bfloat16

RANK = 32
RING = 8
ROWS = 512
WID = 2048
LANES = 128
CHUNKS = 4
CHUNK_ROWS = ROWS // CHUNKS
BLOCK = 4


def mix(a, b, dims):
    return lax.dot_general(a, b, (dims, ((), ())), preferred_element_type=F32)


def mix_exact(a, b, dims):
    return lax.dot_general(
        a, b, (dims, ((), ())), precision=HIGHEST, preferred_element_type=F32
    )


def inverse_lower(packed):
    lane = lax.broadcasted_iota(jnp.int32, (8, LANES), 1)
    row = lax.broadcasted_iota(jnp.int32, (8, LANES), 0)
    parts = []
    for j in range(4):
        shift = (RANK - RANK * j) % LANES
        moved = packed if shift == 0 else pltpu.roll(packed, shift, 1)
        unit = (lane == row + 8 * j).astype(F32)
        parts.append(jnp.where(lane < RANK, unit, jnp.where(lane < 2 * RANK, moved, 0.0)))
    for k in range(0, RANK, BLOCK):
        own, top = k // 8, k % 8
        columns = [
            [
                jnp.broadcast_to(parts[i][:, RANK + k + c : RANK + k + c + 1], (8, LANES))
                for i in range(own, 4)
            ]
            for c in range(BLOCK)
        ]
        rows = [parts[own][top + c : top + c + 1, :] for c in range(BLOCK)]
        for c in range(BLOCK):
            head = columns[c][0]
            inverse = 1.0 / head[top + c : top + c + 1, :]
            scaled = rows[c] * inverse
            for d in range(c + 1, BLOCK):
                entry = head[top + d : top + d + 1, :]
                ratio = entry * inverse
                rows[d] = rows[d] - entry * scaled
                columns[d] = [u - v * ratio for u, v in zip(columns[d], columns[c])]
            for i in range(own, 4):
                column = columns[c][i - own]
                if i == own:
                    column = jnp.where(row > top + c, column, 0.0)
                parts[i] = parts[i] - column * scaled
    done = []
    for j in range(4):
        diagonal = jnp.sum(
            jnp.where(lane == row + RANK + 8 * j, parts[j], 0.0), axis=1, keepdims=True
        )
        done.append(jnp.where(lane < RANK, parts[j] / jnp.sqrt(diagonal), 0.0))
    return jnp.concatenate(done, axis=0)


def kernel(
    w_hbm,
    warm_ref,
    signed_ref,
    pair_ref,
    new_ref,
    wbuf,
    wside,
    fbuf,
    fprior,
    bprior,
    raw,
    halves,
    partial,
    arrived,
    gram_own,
    gram_all,
    gram_plane,
    gram_far,
    plane,
    far,
    summed,
    basis,
    w_sem,
    ws_sem,
    wr_sem,
    gs_sem,
    gr_sem,
    ps_sem,
    pr_sem,
    zs_sem,
    zr_sem,
    zgs_sem,
    zgr_sem,
    fs_sem,
    fr_sem,
    es_sem,
    er_sem,
    bs_sem,
    br_sem,
    hs_sem,
    hr_sem,
):
    blk = lax.axis_index("blk")
    shard = lax.axis_index("shard")
    blks = lax.axis_size("blk")
    x = shard // 4
    far_half = lax.rem(shard // 2, 2)
    core = lax.rem(shard, 2)
    place = 2 * x + core
    above = lax.rem(blk + 1, blks)
    below = lax.rem(blk + blks - 1, blks)
    across = 4 * x + 2 * (1 - far_half) + core
    turns_up = lax.rem(blk, RING) // (RING - 1)
    turns_down = (RING - 1 - lax.rem(blk, RING)) // (RING - 1)
    half_up = lax.rem(far_half + turns_up, 2)
    half_down = lax.rem(far_half + turns_down, 2)
    shard_up = 4 * x + 2 * half_up + core
    shard_down = 4 * x + 2 * half_down + core

    def mate(dx, dc):
        return 4 * lax.rem(x + dx, 4) + 2 * far_half + lax.rem(core + dc, 2)

    others = [(dx, dc) for dx in (2, 1, 3, 0) for dc in (0, 1) if dx or dc]

    def remote(src, dst, send, recv, to_blk, to_shard):
        return pltpu.make_async_remote_copy(
            src_ref=src,
            dst_ref=dst,
            send_sem=send,
            recv_sem=recv,
            device_id=(to_blk, to_shard),
            device_id_type=MESH,
        )

    barrier = pltpu.get_barrier_semaphore()
    greeted = [(below, shard), (above, shard), (blk, across), (above, shard_up), (below, shard_down)]
    greeted += [(blk, mate(dx, dc)) for dx, dc in others]
    for peer in greeted:
        pl.semaphore_signal(barrier, inc=1, device_id=peer, device_id_type=MESH)

    def load(c):
        return pltpu.make_async_copy(
            w_hbm.at[pl.ds(c * CHUNK_ROWS, CHUNK_ROWS), :],
            wbuf.at[pl.ds(2 * c * CHUNK_ROWS, CHUNK_ROWS), :],
            w_sem.at[c],
        )

    for c in range(CHUNKS):
        load(c).start()
    for q in range(16):
        fbuf[q] = warm_ref[:, q * LANES : (q + 1) * LANES].astype(BF16)
    raw[...] = jnp.zeros_like(raw)
    summed[...] = jnp.zeros_like(summed)
    pl.semaphore_wait(barrier, len(greeted))

    def weight_copy(c):
        rows = pl.ds(c * CHUNK_ROWS, CHUNK_ROWS)
        return remote(
            w_hbm.at[rows, :],
            wbuf.at[pl.ds((2 * c + 1) * CHUNK_ROWS, CHUNK_ROWS), :],
            ws_sem.at[c],
            wr_sem.at[c],
            below,
            shard,
        )

    for c in range(CHUNKS):
        weight_copy(c).start()

    def turn(part):
        start = pl.multiple_of(part * CHUNK_ROWS, CHUNK_ROWS)
        for q in range(16):
            wside[q * LANES : (q + 1) * LANES, pl.ds(start, CHUNK_ROWS)] = wbuf[
                pl.ds(start, CHUNK_ROWS), q * LANES : (q + 1) * LANES
            ].T

    partial[...] = jnp.zeros_like(partial)
    for c in range(CHUNKS):
        load(c).wait()
        turn(2 * c)

    lane8 = lax.broadcasted_iota(jnp.int32, (8, LANES), 1) // RANK

    def gram_copy(dx, dc):
        t = 2 * dx + dc
        return remote(
            gram_own, gram_all.at[place], gs_sem.at[t], gr_sem.at[t], blk, mate(dx, dc)
        )

    def part_copy(j, dx, dc):
        t = 2 * dx + dc
        return remote(
            partial.at[j, t], arrived.at[j, t], ps_sem.at[j, t], pr_sem.at[j, t], blk, mate(dx, dc)
        )

    def gather_copy(j, dx, dc):
        t = 2 * dx + dc
        q = 4 * x + 2 * j + core
        return remote(
            fbuf.at[q], fbuf.at[q], fs_sem.at[j, t], fr_sem.at[j, t], blk, mate(dx, dc)
        )

    def far_gram_copy(slot):
        return remote(gram_plane.at[slot], gram_far.at[slot], zgs_sem.at[slot], zgr_sem.at[slot], blk, across)

    def far_copy(slot, j):
        return remote(plane.at[slot, j], far.at[slot, j], zs_sem.at[slot, j], zr_sem.at[slot, j], blk, across)

    def up_copy(j):
        q = 4 * x + 2 * j + core
        return remote(fbuf.at[q], fprior.at[q], es_sem.at[j], er_sem.at[j], above, shard_up)

    def pass_copy(j, dx, dc):
        t = 2 * dx + dc
        q = 4 * x + 2 * j + core
        return remote(
            fprior.at[q], fprior.at[q], hs_sem.at[j, t], hr_sem.at[j, t], blk, mate(dx, dc)
        )

    basis_copy = remote(basis, bprior, bs_sem, br_sem, above, shard)

    def send_gram():
        raw_now = raw[0:RANK, :]
        stacked = jnp.concatenate([raw_now] * 4, axis=0)
        gram4 = mix_exact(raw_now, stacked, ((1,), (1,)))
        packed = gram4[0:8]
        for j in range(1, 4):
            packed = jnp.where(lane8 == j, gram4[8 * j : 8 * j + 8], packed)
        gram_own[...] = packed
        gram_all[place] = packed
        for dx, dc in others:
            gram_copy(dx, dc).start()

    def keep_halves(value, start):
        high = value.astype(BF16)
        low = (value - high.astype(F32)).astype(BF16)
        here, there = pl.ds(start, CHUNK_ROWS), pl.ds(start + CHUNK_ROWS, CHUNK_ROWS)
        halves[0:RANK, here] = high
        halves[0:RANK, there] = -high
        halves[RANK:, here] = low
        halves[RANK:, there] = -low

    def product(rows, j, dx):
        start = pl.multiple_of(512 * lax.rem(x + dx, 4) + 256 * j, 256)
        both = mix(halves[:, rows], wbuf[rows, pl.ds(start, 256)], ((1,), (0,)))
        piece = both[:RANK] + both[RANK:]
        return (2 * dx + core, piece[:, :LANES]), (2 * dx + 1 - core, piece[:, LANES:])

    def send_parts(j, dx):
        for dc in (0, 1):
            if dx or dc:
                part_copy(j, dx, dc).start()

    order = [(j, dx) for j in range(2) for dx in (2, 1, 3, 0)]

    first_factor = jnp.concatenate([fbuf[q] for q in range(16)], axis=1)

    def first_chunk(c, carry):
        weight_copy(c).wait_recv()
        turn(2 * c + 1)
        start = pl.multiple_of(2 * CHUNK_ROWS * c, 2 * CHUNK_ROWS)
        rows = pl.ds(start, 2 * CHUNK_ROWS)
        own = mix(first_factor, wside[:, rows], ((1,), (0,)))
        value = own[:, :CHUNK_ROWS] - own[:, CHUNK_ROWS:]
        raw[0:RANK, pl.ds(pl.multiple_of(CHUNK_ROWS * c, CHUNK_ROWS), CHUNK_ROWS)] = value
        keep_halves(value, start)
        for j, dx in order:
            for t, piece in product(rows, j, dx):
                partial[j, t] = partial[j, t] + piece
        return carry

    lax.fori_loop(0, CHUNKS, first_chunk, 0)
    for j, dx in order:
        send_parts(j, dx)
    send_gram()
    for c in range(CHUNKS):
        weight_copy(c).wait_send()

    def forward():
        own = jnp.zeros((RANK, 2 * ROWS), F32)
        for j in range(2):
            for dx, dc in others:
                gather_copy(j, dx, dc).wait()
            for q in range(2 * j, 16, 4):
                factor = jnp.concatenate([fbuf[q], fbuf[q + 1]], axis=1)
                own = own + mix(factor, wside[q * LANES : (q + 2) * LANES, :], ((1,), (0,)))
        for c in range(CHUNKS):
            start = 2 * CHUNK_ROWS * c
            middle, end = start + CHUNK_ROWS, start + 2 * CHUNK_ROWS
            value = own[:, start:middle] - own[:, middle:end]
            raw[0:RANK, CHUNK_ROWS * c : CHUNK_ROWS * (c + 1)] = value
            keep_halves(value, start)
        send_gram()
        for j, dx in order:
            for t, piece in product(slice(None), j, dx):
                partial[j, t] = piece
            send_parts(j, dx)

    def step(k, carry):
        slot = lax.rem(k, 2)
        for dx, dc in others:
            gram_copy(dx, dc).wait_recv()
        gram_plane[slot] = jnp.sum(gram_all[...], axis=0)
        far_gram_copy(slot).start()
        for j in range(2):
            total = partial[j, 0]
            for dx, dc in others:
                part_copy(j, dx, dc).wait_recv()
            for t in range(1, 8):
                total = total + arrived[j, t]
            plane[slot, j] = total
            far_copy(slot, j).start()
        far_gram_copy(slot).wait_recv()
        lower_inv = inverse_lower(gram_plane[slot] + gram_far[slot])

        @pl.when(k == POWER - 1)
        def _():
            basis[...] = mix_exact(lower_inv, raw[...], ((1,), (0,))).astype(BF16)
            basis_copy.start()

        for dx, dc in others:
            for j in range(2):
                part_copy(j, dx, dc).wait_send()
        for j in range(2):
            far_copy(slot, j).wait_recv()
            summed[0:RANK, :] = plane[slot, j] + far[slot, j]
            piece = mix_exact(lower_inv, summed[...], ((1,), (0,)))
            fbuf[4 * x + 2 * j + core] = piece.astype(BF16)

            @pl.when(k == POWER - 1)
            def _():
                @pl.when(far_half == j)
                def _():
                    new_ref[...] = piece

                up_copy(j).start()

            for dx, dc in others:
                gather_copy(j, dx, dc).start()
        for dx, dc in others:
            gram_copy(dx, dc).wait_send()
        far_gram_copy(slot).wait_send()
        for j in range(2):
            far_copy(slot, j).wait_send()
        pl.when(k < POWER - 1)(forward)
        return carry

    lax.fori_loop(0, POWER, step, 0)

    for j in range(2):
        for dx, dc in others:
            gather_copy(j, dx, dc).wait()
    for j in range(2):
        up_copy(j).wait_recv()
        for dx, dc in others:
            pass_copy(j, dx, dc).start()
    for q in range(16):
        pair_ref[RANK:, q * LANES : (q + 1) * LANES] = fbuf[q]
    signed_ref[RANK:, :] = -basis[...]
    basis_copy.wait_recv()
    signed_ref[0:RANK, :] = bprior[...]
    for j in range(2):
        for dx, dc in others:
            pass_copy(j, dx, dc).wait()
    for q in range(16):
        pair_ref[0:RANK, q * LANES : (q + 1) * LANES] = fprior[q]
    basis_copy.wait_send()
    for j in range(2):
        up_copy(j).wait_send()


def update_kernel(signed_ref, pair_ref, w_ref, factor_ref, out_ref, new_ref):
    delta = mix(signed_ref[...], pair_ref[...], ((0,), (0,)))
    out_ref[0] = (w_ref[...].astype(F32) + MIXING * delta).astype(BF16)
    new_ref[0] = factor_ref[...]


def on_device(weights, warm_factor):
    local_weight = weights[0]
    vmem = pl.BlockSpec(memory_space=pltpu.VMEM)
    dma = pltpu.SemaphoreType.DMA
    signed, factor_pair, new_factor = pl.pallas_call(
        kernel,
        out_shape=(
            jax.ShapeDtypeStruct((2 * RANK, ROWS), BF16),
            jax.ShapeDtypeStruct((2 * RANK, WID), BF16),
            jax.ShapeDtypeStruct((RANK, LANES), F32),
        ),
        in_specs=[pl.BlockSpec(memory_space=pl.ANY), vmem],
        out_specs=(vmem, vmem, vmem),
        scratch_shapes=[
            pltpu.VMEM((2 * ROWS, WID), BF16),
            pltpu.VMEM((WID, 2 * ROWS), BF16),
            pltpu.VMEM((16, RANK, LANES), BF16),
            pltpu.VMEM((16, RANK, LANES), BF16),
            pltpu.VMEM((RANK, ROWS), BF16),
            pltpu.VMEM((LANES, ROWS), F32),
            pltpu.VMEM((2 * RANK, 2 * ROWS), BF16),
            pltpu.VMEM((2, 8, RANK, LANES), F32),
            pltpu.VMEM((2, 8, RANK, LANES), F32),
            pltpu.VMEM((8, LANES), F32),
            pltpu.VMEM((8, 8, LANES), F32),
            pltpu.VMEM((2, 8, LANES), F32),
            pltpu.VMEM((2, 8, LANES), F32),
            pltpu.VMEM((2, 2, RANK, LANES), F32),
            pltpu.VMEM((2, 2, RANK, LANES), F32),
            pltpu.VMEM((LANES, LANES), F32),
            pltpu.VMEM((RANK, ROWS), BF16),
            dma((CHUNKS,)),
            dma((CHUNKS,)),
            dma((CHUNKS,)),
            dma((8,)),
            dma((8,)),
            dma((2, 8)),
            dma((2, 8)),
            dma((2, 2)),
            dma((2, 2)),
            dma((2,)),
            dma((2,)),
            dma((2, 8)),
            dma((2, 8)),
            dma((2,)),
            dma((2,)),
            dma,
            dma,
            dma((2, 8)),
            dma((2, 8)),
        ],
        compiler_params=pltpu.CompilerParams(collective_id=0, has_side_effects=True),
        name="power_rounds",
    )(local_weight, warm_factor[0])
    columns = 512
    new_weight, new_factor = pl.pallas_call(
        update_kernel,
        grid=(WID // columns,),
        out_shape=(
            jax.ShapeDtypeStruct((1, ROWS, WID), BF16),
            jax.ShapeDtypeStruct((1, RANK, LANES), F32),
        ),
        in_specs=[
            pl.BlockSpec((2 * RANK, ROWS), lambda i: (0, 0)),
            pl.BlockSpec((2 * RANK, columns), lambda i: (0, i)),
            pl.BlockSpec((ROWS, columns), lambda i: (0, i)),
            pl.BlockSpec((RANK, LANES), lambda i: (0, 0)),
        ],
        out_specs=(
            pl.BlockSpec((1, ROWS, columns), lambda i: (0, 0, i)),
            pl.BlockSpec((1, RANK, LANES), lambda i: (0, 0, 0)),
        ),
        name="update",
    )(signed, factor_pair, local_weight, new_factor)
    return new_weight, new_factor


def solution(mesh):
    return jax.shard_map(
        on_device,
        mesh=mesh,
        in_specs=(P("blk", "shard", None), P("blk", None, None)),
        out_specs=(P("blk", "shard", None), P("blk", None, "shard")),
        check_vma=False,
    )
```

```python
import jax
import jax.numpy as jnp
from jax import lax
from jax.experimental import pallas as pl
from jax.experimental.pallas import tpu as pltpu
from jax.sharding import PartitionSpec as P

POWER = 4
MIXING = 1.0 / 3.0
MESH = pl.DeviceIdType.MESH
HIGHEST = lax.Precision.HIGHEST
F32 = jnp.float32
BF16 = jnp.bfloat16

RANK = 32
RING = 8
ROWS = 512
WID = 2048
LANES = 128
CHUNKS = 4
CHUNK_ROWS = ROWS // CHUNKS
BLOCK = 4


def mix(a, b, dims):
    return lax.dot_general(a, b, (dims, ((), ())), preferred_element_type=F32)


def mix_exact(a, b, dims):
    return lax.dot_general(
        a, b, (dims, ((), ())), precision=HIGHEST, preferred_element_type=F32
    )


def inverse_lower(packed):
    lane = lax.broadcasted_iota(jnp.int32, (8, LANES), 1)
    row = lax.broadcasted_iota(jnp.int32, (8, LANES), 0)
    parts = []
    for j in range(4):
        shift = (RANK - RANK * j) % LANES
        moved = packed if shift == 0 else pltpu.roll(packed, shift, 1)
        unit = (lane == row + 8 * j).astype(F32)
        parts.append(jnp.where(lane < RANK, unit, jnp.where(lane < 2 * RANK, moved, 0.0)))
    for k in range(0, RANK, BLOCK):
        own, top = k // 8, k % 8
        columns = [
            [
                jnp.broadcast_to(parts[i][:, RANK + k + c : RANK + k + c + 1], (8, LANES))
                for i in range(own, 4)
            ]
            for c in range(BLOCK)
        ]
        rows = [parts[own][top + c : top + c + 1, :] for c in range(BLOCK)]
        for c in range(BLOCK):
            head = columns[c][0]
            inverse = 1.0 / head[top + c : top + c + 1, :]
            scaled = rows[c] * inverse
            for d in range(c + 1, BLOCK):
                entry = head[top + d : top + d + 1, :]
                ratio = entry * inverse
                rows[d] = rows[d] - entry * scaled
                columns[d] = [u - v * ratio for u, v in zip(columns[d], columns[c])]
            for i in range(own, 4):
                column = columns[c][i - own]
                if i == own:
                    column = jnp.where(row > top + c, column, 0.0)
                parts[i] = parts[i] - column * scaled
    done = []
    for j in range(4):
        diagonal = jnp.sum(
            jnp.where(lane == row + RANK + 8 * j, parts[j], 0.0), axis=1, keepdims=True
        )
        done.append(jnp.where(lane < RANK, parts[j] / jnp.sqrt(diagonal), 0.0))
    return jnp.concatenate(done, axis=0)


def kernel(
    w_hbm,
    warm_ref,
    signed_ref,
    pair_ref,
    new_ref,
    wbuf,
    wside,
    fbuf,
    fprior,
    bprior,
    raw,
    halves,
    partial,
    arrived,
    gram_own,
    gram_all,
    gram_plane,
    gram_far,
    plane,
    far,
    summed,
    basis,
    first_prior,
    own_product,
    prior_product,
    above_product,
    below_product,
    both_halves,
    partial_prior,
    arrived_prior,
    sum_prior,
    sum_above,
    w_sem,
    ws_sem,
    wr_sem,
    gs_sem,
    gr_sem,
    ps_sem,
    pr_sem,
    zs_sem,
    zr_sem,
    zgs_sem,
    zgr_sem,
    fs_sem,
    fr_sem,
    es_sem,
    er_sem,
    bs_sem,
    br_sem,
    hs_sem,
    hr_sem,
    us_sem,
    ur_sem,
    vs_sem,
    vr_sem,
    os_sem,
    or_sem,
    qs_sem,
    qr_sem,
    ds_sem,
    dr_sem,
):
    blk = lax.axis_index("blk")
    shard = lax.axis_index("shard")
    blks = lax.axis_size("blk")
    x = shard // 4
    far_half = lax.rem(shard // 2, 2)
    core = lax.rem(shard, 2)
    place = 2 * x + core
    above = lax.rem(blk + 1, blks)
    below = lax.rem(blk + blks - 1, blks)
    across = 4 * x + 2 * (1 - far_half) + core
    turns_up = lax.rem(blk, RING) // (RING - 1)
    turns_down = (RING - 1 - lax.rem(blk, RING)) // (RING - 1)
    half_up = lax.rem(far_half + turns_up, 2)
    half_down = lax.rem(far_half + turns_down, 2)
    shard_up = 4 * x + 2 * half_up + core
    shard_down = 4 * x + 2 * half_down + core

    def mate(dx, dc):
        return 4 * lax.rem(x + dx, 4) + 2 * far_half + lax.rem(core + dc, 2)

    others = [(dx, dc) for dx in (2, 1, 3, 0) for dc in (0, 1) if dx or dc]

    def remote(src, dst, send, recv, to_blk, to_shard):
        return pltpu.make_async_remote_copy(
            src_ref=src,
            dst_ref=dst,
            send_sem=send,
            recv_sem=recv,
            device_id=(to_blk, to_shard),
            device_id_type=MESH,
        )

    barrier = pltpu.get_barrier_semaphore()
    greeted = [(below, shard), (above, shard), (blk, across), (above, shard_up), (below, shard_down)]
    greeted += [(blk, mate(dx, dc)) for dx, dc in others]
    for peer in greeted:
        pl.semaphore_signal(barrier, inc=1, device_id=peer, device_id_type=MESH)

    def load(c):
        return pltpu.make_async_copy(
            w_hbm.at[pl.ds(c * CHUNK_ROWS, CHUNK_ROWS), :],
            wbuf.at[pl.ds(2 * c * CHUNK_ROWS, CHUNK_ROWS), :],
            w_sem.at[c],
        )

    for c in range(CHUNKS):
        load(c).start()
    for q in range(16):
        fbuf[q] = warm_ref[:, q * LANES : (q + 1) * LANES].astype(BF16)
    raw[...] = jnp.zeros_like(raw)
    summed[...] = jnp.zeros_like(summed)
    pl.semaphore_wait(barrier, len(greeted))

    def weight_copy(c):
        rows = pl.ds(c * CHUNK_ROWS, CHUNK_ROWS)
        return remote(
            w_hbm.at[rows, :],
            wbuf.at[pl.ds((2 * c + 1) * CHUNK_ROWS, CHUNK_ROWS), :],
            ws_sem.at[c],
            wr_sem.at[c],
            below,
            shard,
        )

    def lift_copy(j):
        q = 4 * x + 2 * j + core
        return remote(fbuf.at[q], first_prior.at[q], us_sem.at[j], ur_sem.at[j], above, shard_up)

    def spread_copy(j, dx, dc):
        t = 2 * dx + dc
        q = 4 * x + 2 * j + core
        return remote(
            first_prior.at[q], first_prior.at[q], vs_sem.at[j, t], vr_sem.at[j, t], blk, mate(dx, dc)
        )

    def prior_copy(j, dx, dc):
        t = 2 * dx + dc
        return remote(
            partial_prior.at[j, t],
            arrived_prior.at[j, t],
            qs_sem.at[j, t],
            qr_sem.at[j, t],
            blk,
            mate(dx, dc),
        )

    def down_copy(j):
        return remote(sum_prior.at[j], sum_above.at[j], ds_sem.at[j], dr_sem.at[j], below, shard_down)

    own_copy = remote(own_product, below_product, os_sem.at[0], or_sem.at[0], above, shard)
    other_copy = remote(prior_product, above_product, os_sem.at[1], or_sem.at[1], below, shard)

    for j in range(2):
        lift_copy(j).start()
    weight_copy(0).start()

    def turn(part):
        start = pl.multiple_of(part * CHUNK_ROWS, CHUNK_ROWS)
        for q in range(16):
            wside[q * LANES : (q + 1) * LANES, pl.ds(start, CHUNK_ROWS)] = wbuf[
                pl.ds(start, CHUNK_ROWS), q * LANES : (q + 1) * LANES
            ].T

    for c in range(CHUNKS):
        load(c).wait()
        turn(2 * c)

    lane8 = lax.broadcasted_iota(jnp.int32, (8, LANES), 1) // RANK

    def gram_copy(dx, dc):
        t = 2 * dx + dc
        return remote(
            gram_own, gram_all.at[place], gs_sem.at[t], gr_sem.at[t], blk, mate(dx, dc)
        )

    def part_copy(j, dx, dc):
        t = 2 * dx + dc
        return remote(
            partial.at[j, t], arrived.at[j, t], ps_sem.at[j, t], pr_sem.at[j, t], blk, mate(dx, dc)
        )

    def gather_copy(j, dx, dc):
        t = 2 * dx + dc
        q = 4 * x + 2 * j + core
        return remote(
            fbuf.at[q], fbuf.at[q], fs_sem.at[j, t], fr_sem.at[j, t], blk, mate(dx, dc)
        )

    def far_gram_copy(slot):
        return remote(gram_plane.at[slot], gram_far.at[slot], zgs_sem.at[slot], zgr_sem.at[slot], blk, across)

    def far_copy(slot, j):
        return remote(plane.at[slot, j], far.at[slot, j], zs_sem.at[slot, j], zr_sem.at[slot, j], blk, across)

    def up_copy(j):
        q = 4 * x + 2 * j + core
        return remote(fbuf.at[q], fprior.at[q], es_sem.at[j], er_sem.at[j], above, shard_up)

    def pass_copy(j, dx, dc):
        t = 2 * dx + dc
        q = 4 * x + 2 * j + core
        return remote(
            fprior.at[q], fprior.at[q], hs_sem.at[j, t], hr_sem.at[j, t], blk, mate(dx, dc)
        )

    basis_copy = remote(basis, bprior, bs_sem, br_sem, above, shard)

    def send_gram():
        raw_now = raw[0:RANK, :]
        stacked = jnp.concatenate([raw_now] * 4, axis=0)
        gram4 = mix_exact(raw_now, stacked, ((1,), (1,)))
        packed = gram4[0:8]
        for j in range(1, 4):
            packed = jnp.where(lane8 == j, gram4[8 * j : 8 * j + 8], packed)
        gram_own[...] = packed
        gram_all[place] = packed
        for dx, dc in others:
            gram_copy(dx, dc).start()

    def keep_halves(value, start):
        high = value.astype(BF16)
        low = (value - high.astype(F32)).astype(BF16)
        here, there = pl.ds(start, CHUNK_ROWS), pl.ds(start + CHUNK_ROWS, CHUNK_ROWS)
        halves[0:RANK, here] = high
        halves[0:RANK, there] = -high
        halves[RANK:, here] = low
        halves[RANK:, there] = -low

    def product(rows, j, dx):
        start = pl.multiple_of(512 * lax.rem(x + dx, 4) + 256 * j, 256)
        both = mix(halves[:, rows], wbuf[rows, pl.ds(start, 256)], ((1,), (0,)))
        piece = both[:RANK] + both[RANK:]
        return (2 * dx + core, piece[:, :LANES]), (2 * dx + 1 - core, piece[:, LANES:])

    def send_parts(j, dx):
        for dc in (0, 1):
            if dx or dc:
                part_copy(j, dx, dc).start()

    order = [(j, dx) for j in range(2) for dx in (2, 1, 3, 0)]

    def own_rows_product(factors):
        factor = jnp.concatenate([factors[q] for q in range(16)], axis=1)
        return jnp.concatenate(
            [
                mix(factor, wside[:, 2 * c * CHUNK_ROWS : (2 * c + 1) * CHUNK_ROWS], ((1,), (0,)))
                for c in range(CHUNKS)
            ],
            axis=1,
        )

    own_product[...] = own_rows_product(fbuf)
    own_copy.start()
    for j in range(2):
        lift_copy(j).wait_recv()
        for dx, dc in others:
            spread_copy(j, dx, dc).start()
    for j in range(2):
        for dx, dc in others:
            spread_copy(j, dx, dc).wait_recv()
    prior_product[...] = own_rows_product(first_prior)
    other_copy.start()
    for c in range(1, CHUNKS):
        weight_copy(c).start()
    other_copy.wait_recv()
    raw_own = own_product[...] - above_product[...]
    raw[0:RANK, :] = raw_own
    send_gram()
    own_copy.wait_recv()
    raw_prior = below_product[...] - prior_product[...]
    for place_in, value in ((0, raw_own), (2 * RANK, -raw_prior)):
        high = value.astype(BF16)
        both_halves[place_in : place_in + RANK, :] = high
        both_halves[place_in + RANK : place_in + 2 * RANK, :] = (value - high.astype(F32)).astype(BF16)
    for j, dx in order:
        start = pl.multiple_of(512 * lax.rem(x + dx, 4) + 256 * j, 256)
        both = jnp.zeros((4 * RANK, 256), F32)
        for c in range(CHUNKS):
            here = slice(2 * c * CHUNK_ROWS, (2 * c + 1) * CHUNK_ROWS)
            left = both_halves[:, c * CHUNK_ROWS : (c + 1) * CHUNK_ROWS]
            both = both + mix(left, wbuf[here, pl.ds(start, 256)], ((1,), (0,)))
        piece = both[:RANK] + both[RANK : 2 * RANK]
        piece_prior = both[2 * RANK : 3 * RANK] + both[3 * RANK :]
        near, away = 2 * dx + core, 2 * dx + 1 - core
        partial_prior[j, near] = piece_prior[:, :LANES]
        partial_prior[j, away] = piece_prior[:, LANES:]
        partial[j, near] = piece[:, :LANES]
        partial[j, away] = piece[:, LANES:]
        for dc in (0, 1):
            if dx or dc:
                prior_copy(j, dx, dc).start()
                part_copy(j, dx, dc).start()
    for j in range(2):
        total = partial_prior[j, 0]
        for dx, dc in others:
            prior_copy(j, dx, dc).wait_recv()
        for t in range(1, 8):
            total = total + arrived_prior[j, t]
        sum_prior[j] = total
        down_copy(j).start()
        lift_copy(j).wait_send()

    def second_start():
        for j in range(2):
            for dx, dc in others:
                gather_copy(j, dx, dc).wait()
        partial[...] = jnp.zeros_like(partial)

        def chunk(c, carry):
            weight_copy(c).wait_recv()
            turn(2 * c + 1)
            start = pl.multiple_of(2 * CHUNK_ROWS * c, 2 * CHUNK_ROWS)
            rows = pl.ds(start, 2 * CHUNK_ROWS)
            factor = jnp.concatenate([fbuf[q] for q in range(16)], axis=1)
            own = mix(factor, wside[:, rows], ((1,), (0,)))
            value = own[:, :CHUNK_ROWS] - own[:, CHUNK_ROWS:]
            raw[0:RANK, pl.ds(pl.multiple_of(CHUNK_ROWS * c, CHUNK_ROWS), CHUNK_ROWS)] = value
            keep_halves(value, start)
            for j, dx in order:
                for t, piece in product(rows, j, dx):
                    partial[j, t] = partial[j, t] + piece
            return carry

        lax.fori_loop(0, CHUNKS, chunk, 0)
        for j, dx in order:
            send_parts(j, dx)
        send_gram()

    def forward():
        own = jnp.zeros((RANK, 2 * ROWS), F32)
        for j in range(2):
            for dx, dc in others:
                gather_copy(j, dx, dc).wait()
            for q in range(2 * j, 16, 4):
                factor = jnp.concatenate([fbuf[q], fbuf[q + 1]], axis=1)
                own = own + mix(factor, wside[q * LANES : (q + 2) * LANES, :], ((1,), (0,)))
        for c in range(CHUNKS):
            start = 2 * CHUNK_ROWS * c
            middle, end = start + CHUNK_ROWS, start + 2 * CHUNK_ROWS
            value = own[:, start:middle] - own[:, middle:end]
            raw[0:RANK, CHUNK_ROWS * c : CHUNK_ROWS * (c + 1)] = value
            keep_halves(value, start)
        send_gram()
        for j, dx in order:
            for t, piece in product(slice(None), j, dx):
                partial[j, t] = piece
            send_parts(j, dx)

    def step(k, carry):
        slot = lax.rem(k, 2)
        for dx, dc in others:
            gram_copy(dx, dc).wait_recv()
        gram_plane[slot] = jnp.sum(gram_all[...], axis=0)
        far_gram_copy(slot).start()
        for j in range(2):
            total = partial[j, 0]
            for dx, dc in others:
                part_copy(j, dx, dc).wait_recv()
            for t in range(1, 8):
                total = total + arrived[j, t]
            plane[slot, j] = total

            @pl.when(k == 0)
            def _():
                down_copy(j).wait_recv()
                plane[slot, j] = plane[slot, j] + sum_above[j]

            far_copy(slot, j).start()
        far_gram_copy(slot).wait_recv()
        lower_inv = inverse_lower(gram_plane[slot] + gram_far[slot])

        @pl.when(k == POWER - 1)
        def _():
            basis[...] = mix_exact(lower_inv, raw[...], ((1,), (0,))).astype(BF16)
            basis_copy.start()

        for dx, dc in others:
            for j in range(2):
                part_copy(j, dx, dc).wait_send()
        for j in range(2):
            far_copy(slot, j).wait_recv()
            summed[0:RANK, :] = plane[slot, j] + far[slot, j]
            piece = mix_exact(lower_inv, summed[...], ((1,), (0,)))
            fbuf[4 * x + 2 * j + core] = piece.astype(BF16)

            @pl.when(k == POWER - 1)
            def _():
                @pl.when(far_half == j)
                def _():
                    new_ref[...] = piece

                up_copy(j).start()

            for dx, dc in others:
                gather_copy(j, dx, dc).start()
        for dx, dc in others:
            gram_copy(dx, dc).wait_send()
        far_gram_copy(slot).wait_send()
        for j in range(2):
            far_copy(slot, j).wait_send()
        pl.when(k == 0)(second_start)
        pl.when(jnp.logical_and(k > 0, k < POWER - 1))(forward)
        return carry

    lax.fori_loop(0, POWER, step, 0)

    for j in range(2):
        for dx, dc in others:
            gather_copy(j, dx, dc).wait()
    for j in range(2):
        up_copy(j).wait_recv()
        for dx, dc in others:
            pass_copy(j, dx, dc).start()
    for q in range(16):
        pair_ref[RANK:, q * LANES : (q + 1) * LANES] = fbuf[q]
    signed_ref[RANK:, :] = -basis[...]
    basis_copy.wait_recv()
    signed_ref[0:RANK, :] = bprior[...]
    for j in range(2):
        for dx, dc in others:
            pass_copy(j, dx, dc).wait()
    for q in range(16):
        pair_ref[0:RANK, q * LANES : (q + 1) * LANES] = fprior[q]
    basis_copy.wait_send()
    for j in range(2):
        up_copy(j).wait_send()
    for c in range(CHUNKS):
        weight_copy(c).wait_send()
    own_copy.wait_send()
    other_copy.wait_send()
    for j in range(2):
        down_copy(j).wait_send()
        for dx, dc in others:
            spread_copy(j, dx, dc).wait_send()
            prior_copy(j, dx, dc).wait_send()


def on_device(weights, warm_factor):
    local_weight = weights[0]
    vmem = pl.BlockSpec(memory_space=pltpu.VMEM)
    dma = pltpu.SemaphoreType.DMA
    signed, factor_pair, new_factor = pl.pallas_call(
        kernel,
        out_shape=(
            jax.ShapeDtypeStruct((2 * RANK, ROWS), BF16),
            jax.ShapeDtypeStruct((2 * RANK, WID), BF16),
            jax.ShapeDtypeStruct((RANK, LANES), F32),
        ),
        in_specs=[pl.BlockSpec(memory_space=pl.ANY), vmem],
        out_specs=(vmem, vmem, vmem),
        scratch_shapes=[
            pltpu.VMEM((2 * ROWS, WID), BF16),
            pltpu.VMEM((WID, 2 * ROWS), BF16),
            pltpu.VMEM((16, RANK, LANES), BF16),
            pltpu.VMEM((16, RANK, LANES), BF16),
            pltpu.VMEM((RANK, ROWS), BF16),
            pltpu.VMEM((LANES, ROWS), F32),
            pltpu.VMEM((2 * RANK, 2 * ROWS), BF16),
            pltpu.VMEM((2, 8, RANK, LANES), F32),
            pltpu.VMEM((2, 8, RANK, LANES), F32),
            pltpu.VMEM((8, LANES), F32),
            pltpu.VMEM((8, 8, LANES), F32),
            pltpu.VMEM((2, 8, LANES), F32),
            pltpu.VMEM((2, 8, LANES), F32),
            pltpu.VMEM((2, 2, RANK, LANES), F32),
            pltpu.VMEM((2, 2, RANK, LANES), F32),
            pltpu.VMEM((LANES, LANES), F32),
            pltpu.VMEM((RANK, ROWS), BF16),
            pltpu.VMEM((16, RANK, LANES), BF16),
            pltpu.VMEM((RANK, ROWS), F32),
            pltpu.VMEM((RANK, ROWS), F32),
            pltpu.VMEM((RANK, ROWS), F32),
            pltpu.VMEM((RANK, ROWS), F32),
            pltpu.VMEM((4 * RANK, ROWS), BF16),
            pltpu.VMEM((2, 8, RANK, LANES), F32),
            pltpu.VMEM((2, 8, RANK, LANES), F32),
            pltpu.VMEM((2, RANK, LANES), F32),
            pltpu.VMEM((2, RANK, LANES), F32),
            dma((CHUNKS,)),
            dma((CHUNKS,)),
            dma((CHUNKS,)),
            dma((8,)),
            dma((8,)),
            dma((2, 8)),
            dma((2, 8)),
            dma((2, 2)),
            dma((2, 2)),
            dma((2,)),
            dma((2,)),
            dma((2, 8)),
            dma((2, 8)),
            dma((2,)),
            dma((2,)),
            dma,
            dma,
            dma((2, 8)),
            dma((2, 8)),
            dma((2,)),
            dma((2,)),
            dma((2, 8)),
            dma((2, 8)),
            dma((2,)),
            dma((2,)),
            dma((2, 8)),
            dma((2, 8)),
            dma((2,)),
            dma((2,)),
        ],
        compiler_params=pltpu.CompilerParams(
            collective_id=0, has_side_effects=True, vmem_limit_bytes=48 * 2**20
        ),
        name="power_rounds",
    )(local_weight, warm_factor[0])
    delta = jnp.einsum("jr,jc->rc", signed, factor_pair, preferred_element_type=F32)
    new_weight = (local_weight.astype(F32) + MIXING * delta).astype(BF16)
    return (new_weight[None], new_factor[None])


def solution(mesh):
    return jax.shard_map(
        on_device,
        mesh=mesh,
        in_specs=(P("blk", "shard", None), P("blk", None, None)),
        out_specs=(P("blk", "shard", None), P("blk", None, "shard")),
        check_vma=False,
    )
```

```python
import jax
import jax.numpy as jnp
from jax import lax
from jax.experimental import pallas as pl
from jax.experimental.pallas import tpu as pltpu
from jax.sharding import PartitionSpec as P

POWER = 4
MIXING = 1.0 / 3.0
MESH = pl.DeviceIdType.MESH
HIGHEST = lax.Precision.HIGHEST
F32 = jnp.float32
BF16 = jnp.bfloat16

RANK = 32
RING = 8
ROWS = 512
WID = 2048
LANES = 128
CHUNKS = 4
CHUNK_ROWS = ROWS // CHUNKS
PIECES = 8
PIECE_ROWS = ROWS // PIECES
BLOCK = 4


def mix(a, b, dims):
    return lax.dot_general(a, b, (dims, ((), ())), preferred_element_type=F32)


def mix_exact(a, b, dims):
    return lax.dot_general(
        a, b, (dims, ((), ())), precision=HIGHEST, preferred_element_type=F32
    )


def inverse_lower(packed):
    lane = lax.broadcasted_iota(jnp.int32, (8, LANES), 1)
    row = lax.broadcasted_iota(jnp.int32, (8, LANES), 0)
    parts = []
    for j in range(4):
        shift = (RANK - RANK * j) % LANES
        moved = packed if shift == 0 else pltpu.roll(packed, shift, 1)
        unit = (lane == row + 8 * j).astype(F32)
        parts.append(jnp.where(lane < RANK, unit, jnp.where(lane < 2 * RANK, moved, 0.0)))
    for k in range(0, RANK, BLOCK):
        own, top = k // 8, k % 8
        columns = [
            [
                jnp.broadcast_to(parts[i][:, RANK + k + c : RANK + k + c + 1], (8, LANES))
                for i in range(own, 4)
            ]
            for c in range(BLOCK)
        ]
        rows = [parts[own][top + c : top + c + 1, :] for c in range(BLOCK)]
        for c in range(BLOCK):
            head = columns[c][0]
            inverse = 1.0 / head[top + c : top + c + 1, :]
            scaled = rows[c] * inverse
            for d in range(c + 1, BLOCK):
                entry = head[top + d : top + d + 1, :]
                ratio = entry * inverse
                rows[d] = rows[d] - entry * scaled
                columns[d] = [u - v * ratio for u, v in zip(columns[d], columns[c])]
            for i in range(own, 4):
                column = columns[c][i - own]
                if i == own:
                    column = jnp.where(row > top + c, column, 0.0)
                parts[i] = parts[i] - column * scaled
    done = []
    for j in range(4):
        diagonal = jnp.sum(
            jnp.where(lane == row + RANK + 8 * j, parts[j], 0.0), axis=1, keepdims=True
        )
        done.append(jnp.where(lane < RANK, parts[j] / jnp.sqrt(diagonal), 0.0))
    return jnp.concatenate(done, axis=0)


def kernel(
    w_hbm,
    warm_ref,
    signed_ref,
    pair_ref,
    new_ref,
    wbuf,
    wside,
    fbuf,
    fprior,
    bprior,
    raw,
    halves,
    partial,
    arrived,
    gram_own,
    gram_all,
    gram_plane,
    gram_far,
    plane,
    far,
    summed,
    basis,
    first_prior,
    own_product,
    prior_product,
    above_product,
    below_product,
    both_halves,
    partial_prior,
    arrived_prior,
    sum_prior,
    sum_above,
    w_sem,
    ws_sem,
    wr_sem,
    gs_sem,
    gr_sem,
    ps_sem,
    pr_sem,
    zs_sem,
    zr_sem,
    zgs_sem,
    zgr_sem,
    fs_sem,
    fr_sem,
    es_sem,
    er_sem,
    bs_sem,
    br_sem,
    hs_sem,
    hr_sem,
    us_sem,
    ur_sem,
    vs_sem,
    vr_sem,
    os_sem,
    or_sem,
    qs_sem,
    qr_sem,
    ds_sem,
    dr_sem,
):
    blk = lax.axis_index("blk")
    shard = lax.axis_index("shard")
    blks = lax.axis_size("blk")
    x = shard // 4
    far_half = lax.rem(shard // 2, 2)
    core = lax.rem(shard, 2)
    place = 2 * x + core
    above = lax.rem(blk + 1, blks)
    below = lax.rem(blk + blks - 1, blks)
    across = 4 * x + 2 * (1 - far_half) + core
    turns_up = lax.rem(blk, RING) // (RING - 1)
    turns_down = (RING - 1 - lax.rem(blk, RING)) // (RING - 1)
    half_up = lax.rem(far_half + turns_up, 2)
    half_down = lax.rem(far_half + turns_down, 2)
    shard_up = 4 * x + 2 * half_up + core
    shard_down = 4 * x + 2 * half_down + core

    def mate(dx, dc):
        return 4 * lax.rem(x + dx, 4) + 2 * far_half + lax.rem(core + dc, 2)

    others = [(dx, dc) for dx in (2, 1, 3, 0) for dc in (0, 1) if dx or dc]

    def remote(src, dst, send, recv, to_blk, to_shard):
        return pltpu.make_async_remote_copy(
            src_ref=src,
            dst_ref=dst,
            send_sem=send,
            recv_sem=recv,
            device_id=(to_blk, to_shard),
            device_id_type=MESH,
        )

    barrier = pltpu.get_barrier_semaphore()
    greeted = [(below, shard), (above, shard), (blk, across), (above, shard_up), (below, shard_down)]
    greeted += [(blk, mate(dx, dc)) for dx, dc in others]
    for peer in greeted:
        pl.semaphore_signal(barrier, inc=1, device_id=peer, device_id_type=MESH)

    def load(c):
        return pltpu.make_async_copy(
            w_hbm.at[pl.ds(c * CHUNK_ROWS, CHUNK_ROWS), :],
            wbuf.at[pl.ds(2 * c * CHUNK_ROWS, CHUNK_ROWS), :],
            w_sem.at[c],
        )

    for c in range(CHUNKS):
        load(c).start()
    for q in range(16):
        fbuf[q] = warm_ref[:, q * LANES : (q + 1) * LANES].astype(BF16)
    raw[...] = jnp.zeros_like(raw)
    summed[...] = jnp.zeros_like(summed)
    pl.semaphore_wait(barrier, len(greeted))

    def weight_copy(i):
        first = 2 * (i // 2) * CHUNK_ROWS + CHUNK_ROWS + (i % 2) * PIECE_ROWS
        return remote(
            w_hbm.at[pl.ds(i * PIECE_ROWS, PIECE_ROWS), :],
            wbuf.at[pl.ds(first, PIECE_ROWS), :],
            ws_sem.at[i],
            wr_sem.at[i],
            below,
            shard,
        )

    def lift_copy(j):
        q = 4 * x + 2 * j + core
        return remote(fbuf.at[q], first_prior.at[q], us_sem.at[j], ur_sem.at[j], above, shard_up)

    def spread_copy(j, dx, dc):
        t = 2 * dx + dc
        q = 4 * x + 2 * j + core
        return remote(
            first_prior.at[q], first_prior.at[q], vs_sem.at[j, t], vr_sem.at[j, t], blk, mate(dx, dc)
        )

    def prior_copy(j, dx, dc):
        t = 2 * dx + dc
        return remote(
            partial_prior.at[j, t],
            arrived_prior.at[j, t],
            qs_sem.at[j, t],
            qr_sem.at[j, t],
            blk,
            mate(dx, dc),
        )

    def down_copy(j):
        return remote(sum_prior.at[j], sum_above.at[j], ds_sem.at[j], dr_sem.at[j], below, shard_down)

    own_copy = remote(own_product, below_product, os_sem.at[0], or_sem.at[0], above, shard)
    other_copy = remote(prior_product, above_product, os_sem.at[1], or_sem.at[1], below, shard)

    for j in range(2):
        lift_copy(j).start()
    for i in (0, 1):
        weight_copy(i).start()

    def turn(part):
        start = pl.multiple_of(part * CHUNK_ROWS, CHUNK_ROWS)
        for q in range(16):
            wside[q * LANES : (q + 1) * LANES, pl.ds(start, CHUNK_ROWS)] = wbuf[
                pl.ds(start, CHUNK_ROWS), q * LANES : (q + 1) * LANES
            ].T

    for c in range(CHUNKS):
        load(c).wait()
        turn(2 * c)

    lane8 = lax.broadcasted_iota(jnp.int32, (8, LANES), 1) // RANK

    def gram_copy(dx, dc):
        t = 2 * dx + dc
        return remote(
            gram_own, gram_all.at[place], gs_sem.at[t], gr_sem.at[t], blk, mate(dx, dc)
        )

    def part_copy(j, dx, dc):
        t = 2 * dx + dc
        return remote(
            partial.at[j, t], arrived.at[j, t], ps_sem.at[j, t], pr_sem.at[j, t], blk, mate(dx, dc)
        )

    def gather_copy(j, dx, dc):
        t = 2 * dx + dc
        q = 4 * x + 2 * j + core
        return remote(
            fbuf.at[q], fbuf.at[q], fs_sem.at[j, t], fr_sem.at[j, t], blk, mate(dx, dc)
        )

    def far_gram_copy(slot):
        return remote(gram_plane.at[slot], gram_far.at[slot], zgs_sem.at[slot], zgr_sem.at[slot], blk, across)

    def far_copy(slot, j):
        return remote(plane.at[slot, j], far.at[slot, j], zs_sem.at[slot, j], zr_sem.at[slot, j], blk, across)

    def up_copy(j):
        q = 4 * x + 2 * j + core
        return remote(fbuf.at[q], fprior.at[q], es_sem.at[j], er_sem.at[j], above, shard_up)

    def pass_copy(j, dx, dc):
        t = 2 * dx + dc
        q = 4 * x + 2 * j + core
        return remote(
            fprior.at[q], fprior.at[q], hs_sem.at[j, t], hr_sem.at[j, t], blk, mate(dx, dc)
        )

    basis_copy = remote(basis, bprior, bs_sem, br_sem, above, shard)

    def send_gram():
        raw_now = raw[0:RANK, :]
        stacked = jnp.concatenate([raw_now] * 4, axis=0)
        gram4 = mix_exact(raw_now, stacked, ((1,), (1,)))
        packed = gram4[0:8]
        for j in range(1, 4):
            packed = jnp.where(lane8 == j, gram4[8 * j : 8 * j + 8], packed)
        gram_own[...] = packed
        gram_all[place] = packed
        for dx, dc in others:
            gram_copy(dx, dc).start()

    def keep_halves(value, start):
        high = value.astype(BF16)
        low = (value - high.astype(F32)).astype(BF16)
        here, there = pl.ds(start, CHUNK_ROWS), pl.ds(start + CHUNK_ROWS, CHUNK_ROWS)
        halves[0:RANK, here] = high
        halves[0:RANK, there] = -high
        halves[RANK:, here] = low
        halves[RANK:, there] = -low

    def product(rows, j, dx):
        start = pl.multiple_of(512 * lax.rem(x + dx, 4) + 256 * j, 256)
        both = mix(halves[:, rows], wbuf[rows, pl.ds(start, 256)], ((1,), (0,)))
        piece = both[:RANK] + both[RANK:]
        return (2 * dx + core, piece[:, :LANES]), (2 * dx + 1 - core, piece[:, LANES:])

    def send_parts(j, dx):
        for dc in (0, 1):
            if dx or dc:
                part_copy(j, dx, dc).start()

    order = [(j, dx) for j in range(2) for dx in (2, 1, 3, 0)]

    def own_rows_product(factors):
        factor = jnp.concatenate([factors[q] for q in range(16)], axis=1)
        return jnp.concatenate(
            [
                mix(factor, wside[:, 2 * c * CHUNK_ROWS : (2 * c + 1) * CHUNK_ROWS], ((1,), (0,)))
                for c in range(CHUNKS)
            ],
            axis=1,
        )

    own_product[...] = own_rows_product(fbuf)
    own_copy.start()
    for j in range(2):
        lift_copy(j).wait_recv()
        for dx, dc in others:
            spread_copy(j, dx, dc).start()
    for j in range(2):
        for dx, dc in others:
            spread_copy(j, dx, dc).wait_recv()
    prior_product[...] = own_rows_product(first_prior)
    other_copy.start()
    for i in (2, 3):
        weight_copy(i).start()
    other_copy.wait_recv()
    raw_own = own_product[...] - above_product[...]
    raw[0:RANK, :] = raw_own
    send_gram()
    own_copy.wait_recv()
    raw_prior = below_product[...] - prior_product[...]
    for place_in, value in ((0, raw_own), (2 * RANK, -raw_prior)):
        high = value.astype(BF16)
        both_halves[place_in : place_in + RANK, :] = high
        both_halves[place_in + RANK : place_in + 2 * RANK, :] = (value - high.astype(F32)).astype(BF16)
    for j, dx in order:
        start = pl.multiple_of(512 * lax.rem(x + dx, 4) + 256 * j, 256)
        both = jnp.zeros((4 * RANK, 256), F32)
        for c in range(CHUNKS):
            here = slice(2 * c * CHUNK_ROWS, (2 * c + 1) * CHUNK_ROWS)
            left = both_halves[:, c * CHUNK_ROWS : (c + 1) * CHUNK_ROWS]
            both = both + mix(left, wbuf[here, pl.ds(start, 256)], ((1,), (0,)))
        piece = both[:RANK] + both[RANK : 2 * RANK]
        piece_prior = both[2 * RANK : 3 * RANK] + both[3 * RANK :]
        near, away = 2 * dx + core, 2 * dx + 1 - core
        partial_prior[j, near] = piece_prior[:, :LANES]
        partial_prior[j, away] = piece_prior[:, LANES:]
        partial[j, near] = piece[:, :LANES]
        partial[j, away] = piece[:, LANES:]
        for dc in (0, 1):
            if dx or dc:
                prior_copy(j, dx, dc).start()
                part_copy(j, dx, dc).start()
    for i in (4, 5):
        weight_copy(i).start()
    for j in range(2):
        total = partial_prior[j, 0]
        for dx, dc in others:
            prior_copy(j, dx, dc).wait_recv()
        for t in range(1, 8):
            total = total + arrived_prior[j, t]
        sum_prior[j] = total
        down_copy(j).start()
        lift_copy(j).wait_send()
    for i in (6,):
        weight_copy(i).start()

    def second_start():
        for j in range(2):
            for dx, dc in others:
                gather_copy(j, dx, dc).wait()
        partial[...] = jnp.zeros_like(partial)

        def chunk(c, carry):
            weight_copy(2 * c).wait_recv()
            weight_copy(2 * c + 1).wait_recv()
            turn(2 * c + 1)
            start = pl.multiple_of(2 * CHUNK_ROWS * c, 2 * CHUNK_ROWS)
            rows = pl.ds(start, 2 * CHUNK_ROWS)
            factor = jnp.concatenate([fbuf[q] for q in range(16)], axis=1)
            own = mix(factor, wside[:, rows], ((1,), (0,)))
            value = own[:, :CHUNK_ROWS] - own[:, CHUNK_ROWS:]
            raw[0:RANK, pl.ds(pl.multiple_of(CHUNK_ROWS * c, CHUNK_ROWS), CHUNK_ROWS)] = value
            keep_halves(value, start)
            for j, dx in order:
                for t, piece in product(rows, j, dx):
                    partial[j, t] = partial[j, t] + piece
            return carry

        lax.fori_loop(0, CHUNKS, chunk, 0)
        for j, dx in order:
            send_parts(j, dx)
        send_gram()

    def forward():
        own = jnp.zeros((RANK, 2 * ROWS), F32)
        for j in range(2):
            for dx, dc in others:
                gather_copy(j, dx, dc).wait()
            for q in range(2 * j, 16, 4):
                factor = jnp.concatenate([fbuf[q], fbuf[q + 1]], axis=1)
                own = own + mix(factor, wside[q * LANES : (q + 2) * LANES, :], ((1,), (0,)))
        for c in range(CHUNKS):
            start = 2 * CHUNK_ROWS * c
            middle, end = start + CHUNK_ROWS, start + 2 * CHUNK_ROWS
            value = own[:, start:middle] - own[:, middle:end]
            raw[0:RANK, CHUNK_ROWS * c : CHUNK_ROWS * (c + 1)] = value
            keep_halves(value, start)
        send_gram()
        for j, dx in order:
            for t, piece in product(slice(None), j, dx):
                partial[j, t] = piece
            send_parts(j, dx)

    def step(k, carry):
        slot = lax.rem(k, 2)
        for dx, dc in others:
            gram_copy(dx, dc).wait_recv()
        gram_plane[slot] = jnp.sum(gram_all[...], axis=0)
        far_gram_copy(slot).start()
        for j in range(2):
            total = partial[j, 0]
            for dx, dc in others:
                part_copy(j, dx, dc).wait_recv()
            for t in range(1, 8):
                total = total + arrived[j, t]
            plane[slot, j] = total

            @pl.when(k == 0)
            def _():
                down_copy(j).wait_recv()
                plane[slot, j] = plane[slot, j] + sum_above[j]

            far_copy(slot, j).start()

        @pl.when(k == 0)
        def _():
            for i in (7,):
                weight_copy(i).start()

        far_gram_copy(slot).wait_recv()
        lower_inv = inverse_lower(gram_plane[slot] + gram_far[slot])

        @pl.when(k == POWER - 1)
        def _():
            basis[...] = mix_exact(lower_inv, raw[...], ((1,), (0,))).astype(BF16)
            basis_copy.start()

        for dx, dc in others:
            for j in range(2):
                part_copy(j, dx, dc).wait_send()
        for j in range(2):
            far_copy(slot, j).wait_recv()
            summed[0:RANK, :] = plane[slot, j] + far[slot, j]
            piece = mix_exact(lower_inv, summed[...], ((1,), (0,)))
            fbuf[4 * x + 2 * j + core] = piece.astype(BF16)

            @pl.when(k == POWER - 1)
            def _():
                @pl.when(far_half == j)
                def _():
                    new_ref[...] = piece

                up_copy(j).start()

            for dx, dc in others:
                gather_copy(j, dx, dc).start()
        for dx, dc in others:
            gram_copy(dx, dc).wait_send()
        far_gram_copy(slot).wait_send()
        for j in range(2):
            far_copy(slot, j).wait_send()
        pl.when(k == 0)(second_start)
        pl.when(jnp.logical_and(k > 0, k < POWER - 1))(forward)
        return carry

    lax.fori_loop(0, POWER, step, 0)

    for j in range(2):
        for dx, dc in others:
            gather_copy(j, dx, dc).wait()
    for j in range(2):
        up_copy(j).wait_recv()
        for dx, dc in others:
            pass_copy(j, dx, dc).start()
    for q in range(16):
        pair_ref[RANK:, q * LANES : (q + 1) * LANES] = fbuf[q]
    signed_ref[RANK:, :] = -basis[...]
    basis_copy.wait_recv()
    signed_ref[0:RANK, :] = bprior[...]
    for j in range(2):
        for dx, dc in others:
            pass_copy(j, dx, dc).wait()
    for q in range(16):
        pair_ref[0:RANK, q * LANES : (q + 1) * LANES] = fprior[q]
    basis_copy.wait_send()
    for j in range(2):
        up_copy(j).wait_send()
    for i in range(PIECES):
        weight_copy(i).wait_send()
    own_copy.wait_send()
    other_copy.wait_send()
    for j in range(2):
        down_copy(j).wait_send()
        for dx, dc in others:
            spread_copy(j, dx, dc).wait_send()
            prior_copy(j, dx, dc).wait_send()


def on_device(weights, warm_factor):
    local_weight = weights[0]
    vmem = pl.BlockSpec(memory_space=pltpu.VMEM)
    dma = pltpu.SemaphoreType.DMA
    signed, factor_pair, new_factor = pl.pallas_call(
        kernel,
        out_shape=(
            jax.ShapeDtypeStruct((2 * RANK, ROWS), BF16),
            jax.ShapeDtypeStruct((2 * RANK, WID), BF16),
            jax.ShapeDtypeStruct((RANK, LANES), F32),
        ),
        in_specs=[pl.BlockSpec(memory_space=pl.ANY), vmem],
        out_specs=(vmem, vmem, vmem),
        scratch_shapes=[
            pltpu.VMEM((2 * ROWS, WID), BF16),
            pltpu.VMEM((WID, 2 * ROWS), BF16),
            pltpu.VMEM((16, RANK, LANES), BF16),
            pltpu.VMEM((16, RANK, LANES), BF16),
            pltpu.VMEM((RANK, ROWS), BF16),
            pltpu.VMEM((LANES, ROWS), F32),
            pltpu.VMEM((2 * RANK, 2 * ROWS), BF16),
            pltpu.VMEM((2, 8, RANK, LANES), F32),
            pltpu.VMEM((2, 8, RANK, LANES), F32),
            pltpu.VMEM((8, LANES), F32),
            pltpu.VMEM((8, 8, LANES), F32),
            pltpu.VMEM((2, 8, LANES), F32),
            pltpu.VMEM((2, 8, LANES), F32),
            pltpu.VMEM((2, 2, RANK, LANES), F32),
            pltpu.VMEM((2, 2, RANK, LANES), F32),
            pltpu.VMEM((LANES, LANES), F32),
            pltpu.VMEM((RANK, ROWS), BF16),
            pltpu.VMEM((16, RANK, LANES), BF16),
            pltpu.VMEM((RANK, ROWS), F32),
            pltpu.VMEM((RANK, ROWS), F32),
            pltpu.VMEM((RANK, ROWS), F32),
            pltpu.VMEM((RANK, ROWS), F32),
            pltpu.VMEM((4 * RANK, ROWS), BF16),
            pltpu.VMEM((2, 8, RANK, LANES), F32),
            pltpu.VMEM((2, 8, RANK, LANES), F32),
            pltpu.VMEM((2, RANK, LANES), F32),
            pltpu.VMEM((2, RANK, LANES), F32),
            dma((CHUNKS,)),
            dma((PIECES,)),
            dma((PIECES,)),
            dma((8,)),
            dma((8,)),
            dma((2, 8)),
            dma((2, 8)),
            dma((2, 2)),
            dma((2, 2)),
            dma((2,)),
            dma((2,)),
            dma((2, 8)),
            dma((2, 8)),
            dma((2,)),
            dma((2,)),
            dma,
            dma,
            dma((2, 8)),
            dma((2, 8)),
            dma((2,)),
            dma((2,)),
            dma((2, 8)),
            dma((2, 8)),
            dma((2,)),
            dma((2,)),
            dma((2, 8)),
            dma((2, 8)),
            dma((2,)),
            dma((2,)),
        ],
        compiler_params=pltpu.CompilerParams(
            collective_id=0, has_side_effects=True, vmem_limit_bytes=48 * 2**20
        ),
        name="power_rounds",
    )(local_weight, warm_factor[0])
    delta = jnp.einsum("jr,jc->rc", signed, factor_pair, preferred_element_type=F32)
    new_weight = (local_weight.astype(F32) + MIXING * delta).astype(BF16)
    return (new_weight[None], new_factor[None])


def solution(mesh):
    return jax.shard_map(
        on_device,
        mesh=mesh,
        in_specs=(P("blk", "shard", None), P("blk", None, None)),
        out_specs=(P("blk", "shard", None), P("blk", None, "shard")),
        check_vma=False,
    )
```

```python
import jax
import jax.numpy as jnp
from jax import lax
from jax.experimental import pallas as pl
from jax.experimental.pallas import tpu as pltpu
from jax.sharding import PartitionSpec as P

POWER = 4
MIXING = 1.0 / 3.0
MESH = pl.DeviceIdType.MESH
HIGHEST = lax.Precision.HIGHEST
F32 = jnp.float32
BF16 = jnp.bfloat16

RANK = 32
RING = 8
ROWS = 512
WID = 2048
LANES = 128
CHUNKS = 4
CHUNK_ROWS = ROWS // CHUNKS
PIECES = 8
PIECE_ROWS = ROWS // PIECES
AWAY = (2, 1, 3, 0)
BLOCK = 8


def mix(a, b, dims):
    return lax.dot_general(a, b, (dims, ((), ())), preferred_element_type=F32)


def mix_exact(a, b, dims):
    return lax.dot_general(
        a, b, (dims, ((), ())), precision=HIGHEST, preferred_element_type=F32
    )


def inverse_lower(packed):
    lane = lax.broadcasted_iota(jnp.int32, (8, LANES), 1)
    row = lax.broadcasted_iota(jnp.int32, (8, LANES), 0)
    parts = []
    for j in range(4):
        shift = (RANK - RANK * j) % LANES
        moved = packed if shift == 0 else pltpu.roll(packed, shift, 1)
        unit = (lane == row + 8 * j).astype(F32)
        parts.append(jnp.where(lane < RANK, unit, jnp.where(lane < 2 * RANK, moved, 0.0)))
    for k in range(0, RANK, BLOCK):
        own, top = k // 8, k % 8
        columns = [
            [
                jnp.broadcast_to(parts[i][:, RANK + k + c : RANK + k + c + 1], (8, LANES))
                for i in range(own, 4)
            ]
            for c in range(BLOCK)
        ]
        rows = [parts[own][top + c : top + c + 1, :] for c in range(BLOCK)]
        for c in range(BLOCK):
            head = columns[c][0]
            inverse = 1.0 / head[top + c : top + c + 1, :]
            scaled = rows[c] * inverse
            for d in range(c + 1, BLOCK):
                entry = head[top + d : top + d + 1, :]
                ratio = entry * inverse
                rows[d] = rows[d] - entry * scaled
                columns[d] = [u - v * ratio for u, v in zip(columns[d], columns[c])]
            for i in range(own, 4):
                column = columns[c][i - own]
                if i == own:
                    column = jnp.where(row > top + c, column, 0.0)
                parts[i] = parts[i] - column * scaled
    done = []
    for j in range(4):
        diagonal = jnp.sum(
            jnp.where(lane == row + RANK + 8 * j, parts[j], 0.0), axis=1, keepdims=True
        )
        done.append(jnp.where(lane < RANK, parts[j] / jnp.sqrt(diagonal), 0.0))
    return jnp.concatenate(done, axis=0)


def kernel(
    w_hbm,
    warm_ref,
    signed_ref,
    pair_ref,
    new_ref,
    wbuf,
    wside,
    fbuf,
    fprior,
    bprior,
    raw,
    halves,
    partial,
    arrived,
    gram_own,
    gram_all,
    gram_plane,
    gram_far,
    plane,
    far,
    summed,
    basis,
    first_prior,
    own_product,
    prior_product,
    above_product,
    below_product,
    both_halves,
    partial_prior,
    arrived_prior,
    sum_prior,
    sum_above,
    w_sem,
    ws_sem,
    wr_sem,
    gs_sem,
    gr_sem,
    ps_sem,
    pr_sem,
    zs_sem,
    zr_sem,
    zgs_sem,
    zgr_sem,
    fs_sem,
    fr_sem,
    es_sem,
    er_sem,
    bs_sem,
    br_sem,
    hs_sem,
    hr_sem,
    us_sem,
    ur_sem,
    vs_sem,
    vr_sem,
    os_sem,
    or_sem,
    qs_sem,
    qr_sem,
    ds_sem,
    dr_sem,
):
    blk = lax.axis_index("blk")
    shard = lax.axis_index("shard")
    blks = lax.axis_size("blk")
    x = shard // 4
    far_half = lax.rem(shard // 2, 2)
    core = lax.rem(shard, 2)
    place = 2 * x + core
    above = lax.rem(blk + 1, blks)
    below = lax.rem(blk + blks - 1, blks)
    across = 4 * x + 2 * (1 - far_half) + core
    turns_up = lax.rem(blk, RING) // (RING - 1)
    turns_down = (RING - 1 - lax.rem(blk, RING)) // (RING - 1)
    half_up = lax.rem(far_half + turns_up, 2)
    half_down = lax.rem(far_half + turns_down, 2)
    shard_up = 4 * x + 2 * half_up + core
    shard_down = 4 * x + 2 * half_down + core

    def mate(dx, dc):
        return 4 * lax.rem(x + dx, 4) + 2 * far_half + lax.rem(core + dc, 2)

    others = [(dx, dc) for dx in (2, 1, 3, 0) for dc in (0, 1) if dx or dc]

    def remote(src, dst, send, recv, to_blk, to_shard):
        return pltpu.make_async_remote_copy(
            src_ref=src,
            dst_ref=dst,
            send_sem=send,
            recv_sem=recv,
            device_id=(to_blk, to_shard),
            device_id_type=MESH,
        )

    barrier = pltpu.get_barrier_semaphore()
    greeted = [(below, shard), (above, shard), (blk, across), (above, shard_up), (below, shard_down)]
    greeted += [(blk, mate(dx, dc)) for dx, dc in others]
    for peer in greeted:
        pl.semaphore_signal(barrier, inc=1, device_id=peer, device_id_type=MESH)

    def load(c):
        return pltpu.make_async_copy(
            w_hbm.at[pl.ds(c * CHUNK_ROWS, CHUNK_ROWS), :],
            wbuf.at[pl.ds(2 * c * CHUNK_ROWS, CHUNK_ROWS), :],
            w_sem.at[c],
        )

    for c in range(CHUNKS):
        load(c).start()
    for q in range(16):
        fbuf[q] = warm_ref[:, q * LANES : (q + 1) * LANES].astype(BF16)
    raw[...] = jnp.zeros_like(raw)
    summed[...] = jnp.zeros_like(summed)
    pl.semaphore_wait(barrier, len(greeted))

    def weight_copy(i):
        first = 2 * (i // 2) * CHUNK_ROWS + CHUNK_ROWS + (i % 2) * PIECE_ROWS
        return remote(
            w_hbm.at[pl.ds(i * PIECE_ROWS, PIECE_ROWS), :],
            wbuf.at[pl.ds(first, PIECE_ROWS), :],
            ws_sem.at[i],
            wr_sem.at[i],
            below,
            shard,
        )

    def lift_copy(j):
        q = 4 * x + 2 * j + core
        return remote(fbuf.at[q], first_prior.at[q], us_sem.at[j], ur_sem.at[j], above, shard_up)

    def spread_copy(j, dx, dc):
        t = 2 * dx + dc
        q = 4 * x + 2 * j + core
        return remote(
            first_prior.at[q], first_prior.at[q], vs_sem.at[j, t], vr_sem.at[j, t], blk, mate(dx, dc)
        )

    def prior_copy(j, dx, dc):
        t = 2 * dx + dc
        return remote(
            partial_prior.at[j, t],
            arrived_prior.at[j, t],
            qs_sem.at[j, t],
            qr_sem.at[j, t],
            blk,
            mate(dx, dc),
        )

    def down_copy(j):
        return remote(sum_prior.at[j], sum_above.at[j], ds_sem.at[j], dr_sem.at[j], below, shard_down)

    own_copy = remote(own_product, below_product, os_sem.at[0], or_sem.at[0], above, shard)
    other_copy = remote(prior_product, above_product, os_sem.at[1], or_sem.at[1], below, shard)

    for j in range(2):
        lift_copy(j).start()
    for i in (0, 1):
        weight_copy(i).start()

    def turn(part):
        start = pl.multiple_of(part * CHUNK_ROWS, CHUNK_ROWS)
        for q in range(16):
            wside[q * LANES : (q + 1) * LANES, pl.ds(start, CHUNK_ROWS)] = wbuf[
                pl.ds(start, CHUNK_ROWS), q * LANES : (q + 1) * LANES
            ].T

    for c in range(CHUNKS):
        load(c).wait()
        turn(2 * c)

    lane8 = lax.broadcasted_iota(jnp.int32, (8, LANES), 1) // RANK

    def gram_copy(dx, dc):
        t = 2 * dx + dc
        return remote(
            gram_own, gram_all.at[place], gs_sem.at[t], gr_sem.at[t], blk, mate(dx, dc)
        )

    def part_copy(j, dx, dc):
        t = 2 * dx + dc
        return remote(
            partial.at[j, t], arrived.at[j, t], ps_sem.at[j, t], pr_sem.at[j, t], blk, mate(dx, dc)
        )

    def gather_copy(j, dx, dc):
        t = 2 * dx + dc
        q = 4 * x + 2 * j + core
        return remote(
            fbuf.at[q], fbuf.at[q], fs_sem.at[j, t], fr_sem.at[j, t], blk, mate(dx, dc)
        )

    def far_gram_copy(slot):
        return remote(gram_plane.at[slot], gram_far.at[slot], zgs_sem.at[slot], zgr_sem.at[slot], blk, across)

    def far_copy(slot, j):
        return remote(plane.at[slot, j], far.at[slot, j], zs_sem.at[slot, j], zr_sem.at[slot, j], blk, across)

    def up_copy(j):
        q = 4 * x + 2 * j + core
        return remote(fbuf.at[q], fprior.at[q], es_sem.at[j], er_sem.at[j], above, shard_up)

    def pass_copy(j, dx, dc):
        t = 2 * dx + dc
        q = 4 * x + 2 * j + core
        return remote(
            fprior.at[q], fprior.at[q], hs_sem.at[j, t], hr_sem.at[j, t], blk, mate(dx, dc)
        )

    basis_copy = remote(basis, bprior, bs_sem, br_sem, above, shard)

    def send_gram():
        raw_now = raw[0:RANK, :]
        stacked = jnp.concatenate([raw_now] * 4, axis=0)
        gram4 = mix_exact(raw_now, stacked, ((1,), (1,)))
        packed = gram4[0:8]
        for j in range(1, 4):
            packed = jnp.where(lane8 == j, gram4[8 * j : 8 * j + 8], packed)
        gram_own[...] = packed
        gram_all[place] = packed
        for dx, dc in others:
            gram_copy(dx, dc).start()

    def keep_halves(value, start):
        high = value.astype(BF16)
        low = (value - high.astype(F32)).astype(BF16)
        here, there = pl.ds(start, CHUNK_ROWS), pl.ds(start + CHUNK_ROWS, CHUNK_ROWS)
        halves[0:RANK, here] = high
        halves[0:RANK, there] = -high
        halves[RANK:, here] = low
        halves[RANK:, there] = -low

    def product(rows, j, dx):
        start = pl.multiple_of(512 * lax.rem(x + dx, 4) + 256 * j, 256)
        both = mix(halves[:, rows], wbuf[rows, pl.ds(start, 256)], ((1,), (0,)))
        piece = both[:RANK] + both[RANK:]
        return (2 * dx + core, piece[:, :LANES]), (2 * dx + 1 - core, piece[:, LANES:])

    def send_parts(j, dx):
        for dc in (0, 1):
            if dx or dc:
                part_copy(j, dx, dc).start()

    order = [(j, dx) for j in range(2) for dx in AWAY]

    def own_rows_product(factors):
        factor = jnp.concatenate([factors[q] for q in range(16)], axis=1)
        return jnp.concatenate(
            [
                mix(factor, wside[:, 2 * c * CHUNK_ROWS : (2 * c + 1) * CHUNK_ROWS], ((1,), (0,)))
                for c in range(CHUNKS)
            ],
            axis=1,
        )

    own_product[...] = own_rows_product(fbuf)
    own_copy.start()
    for j in range(2):
        lift_copy(j).wait_recv()
        for dx, dc in others:
            spread_copy(j, dx, dc).start()
    for j in range(2):
        for dx, dc in others:
            spread_copy(j, dx, dc).wait_recv()
    prior_product[...] = own_rows_product(first_prior)
    other_copy.start()
    for i in (2, 3):
        weight_copy(i).start()
    other_copy.wait_recv()
    raw_own = own_product[...] - above_product[...]
    raw[0:RANK, :] = raw_own
    send_gram()
    own_copy.wait_recv()
    raw_prior = below_product[...] - prior_product[...]
    for place_in, value in ((0, raw_own), (2 * RANK, -raw_prior)):
        high = value.astype(BF16)
        both_halves[place_in : place_in + RANK, :] = high
        both_halves[place_in + RANK : place_in + 2 * RANK, :] = (value - high.astype(F32)).astype(BF16)
    for j in range(2):
        for dx in AWAY:
            start = pl.multiple_of(512 * lax.rem(x + dx, 4) + 256 * j, 256)
            both = jnp.zeros((4 * RANK, 256), F32)
            for c in range(CHUNKS):
                here = slice(2 * c * CHUNK_ROWS, (2 * c + 1) * CHUNK_ROWS)
                left = both_halves[:, c * CHUNK_ROWS : (c + 1) * CHUNK_ROWS]
                both = both + mix(left, wbuf[here, pl.ds(start, 256)], ((1,), (0,)))
            piece = both[:RANK] + both[RANK : 2 * RANK]
            piece_prior = both[2 * RANK : 3 * RANK] + both[3 * RANK :]
            near, away = 2 * dx + core, 2 * dx + 1 - core
            partial_prior[j, near] = piece_prior[:, :LANES]
            partial_prior[j, away] = piece_prior[:, LANES:]
            partial[j, near] = piece[:, :LANES]
            partial[j, away] = piece[:, LANES:]
        for dx, dc in others:
            prior_copy(j, dx, dc).start()
            part_copy(j, dx, dc).start()
    for i in (4, 5):
        weight_copy(i).start()
    for j in range(2):
        total = partial_prior[j, 0]
        for dx, dc in others:
            prior_copy(j, dx, dc).wait_recv()
        for t in range(1, 8):
            total = total + arrived_prior[j, t]
        sum_prior[j] = total
        down_copy(j).start()
        lift_copy(j).wait_send()
    for i in (6,):
        weight_copy(i).start()

    def second_start():
        for j in range(2):
            for dx, dc in others:
                gather_copy(j, dx, dc).wait()
        partial[...] = jnp.zeros_like(partial)

        def chunk(c, carry):
            weight_copy(2 * c).wait_recv()
            weight_copy(2 * c + 1).wait_recv()
            turn(2 * c + 1)
            start = pl.multiple_of(2 * CHUNK_ROWS * c, 2 * CHUNK_ROWS)
            rows = pl.ds(start, 2 * CHUNK_ROWS)
            factor = jnp.concatenate([fbuf[q] for q in range(16)], axis=1)
            own = mix(factor, wside[:, rows], ((1,), (0,)))
            value = own[:, :CHUNK_ROWS] - own[:, CHUNK_ROWS:]
            raw[0:RANK, pl.ds(pl.multiple_of(CHUNK_ROWS * c, CHUNK_ROWS), CHUNK_ROWS)] = value
            keep_halves(value, start)
            for j, dx in order:
                for t, piece in product(rows, j, dx):
                    partial[j, t] = partial[j, t] + piece
            return carry

        lax.fori_loop(0, CHUNKS, chunk, 0)
        for j, dx in order:
            send_parts(j, dx)
        send_gram()

    def forward():
        own = jnp.zeros((RANK, 2 * ROWS), F32)
        for j in range(2):
            for dx, dc in others:
                gather_copy(j, dx, dc).wait()
            for q in range(2 * j, 16, 4):
                factor = jnp.concatenate([fbuf[q], fbuf[q + 1]], axis=1)
                own = own + mix(factor, wside[q * LANES : (q + 2) * LANES, :], ((1,), (0,)))
        for c in range(CHUNKS):
            start = 2 * CHUNK_ROWS * c
            middle, end = start + CHUNK_ROWS, start + 2 * CHUNK_ROWS
            value = own[:, start:middle] - own[:, middle:end]
            raw[0:RANK, CHUNK_ROWS * c : CHUNK_ROWS * (c + 1)] = value
            keep_halves(value, start)
        send_gram()
        for j in range(2):
            for dx in AWAY:
                for t, piece in product(slice(None), j, dx):
                    partial[j, t] = piece
            for dx in AWAY:
                send_parts(j, dx)

    def step(k, carry):
        slot = lax.rem(k, 2)
        for dx, dc in others:
            gram_copy(dx, dc).wait_recv()
        gram_plane[slot] = jnp.sum(gram_all[...], axis=0)
        far_gram_copy(slot).start()
        for j in range(2):
            total = partial[j, 0]
            for dx, dc in others:
                part_copy(j, dx, dc).wait_recv()
            for t in range(1, 8):
                total = total + arrived[j, t]
            plane[slot, j] = total

            @pl.when(k == 0)
            def _():
                down_copy(j).wait_recv()
                plane[slot, j] = plane[slot, j] + sum_above[j]

            far_copy(slot, j).start()

        @pl.when(k == 0)
        def _():
            for i in (7,):
                weight_copy(i).start()

        far_gram_copy(slot).wait_recv()
        lower_inv = inverse_lower(gram_plane[slot] + gram_far[slot])

        @pl.when(k == POWER - 1)
        def _():
            basis[...] = mix_exact(lower_inv, raw[...], ((1,), (0,))).astype(BF16)
            basis_copy.start()

        for dx, dc in others:
            for j in range(2):
                part_copy(j, dx, dc).wait_send()
        for j in range(2):
            far_copy(slot, j).wait_recv()
            summed[0:RANK, :] = plane[slot, j] + far[slot, j]
            piece = mix_exact(lower_inv, summed[...], ((1,), (0,)))
            fbuf[4 * x + 2 * j + core] = piece.astype(BF16)

            @pl.when(k == POWER - 1)
            def _():
                @pl.when(far_half == j)
                def _():
                    new_ref[...] = piece

                up_copy(j).start()

            for dx, dc in others:
                gather_copy(j, dx, dc).start()
        for dx, dc in others:
            gram_copy(dx, dc).wait_send()
        far_gram_copy(slot).wait_send()
        for j in range(2):
            far_copy(slot, j).wait_send()
        pl.when(k == 0)(second_start)
        pl.when(jnp.logical_and(k > 0, k < POWER - 1))(forward)
        return carry

    lax.fori_loop(0, POWER, step, 0)

    for j in range(2):
        for dx, dc in others:
            gather_copy(j, dx, dc).wait()
    for j in range(2):
        up_copy(j).wait_recv()
        for dx, dc in others:
            pass_copy(j, dx, dc).start()
    for q in range(16):
        pair_ref[RANK:, q * LANES : (q + 1) * LANES] = fbuf[q]
    signed_ref[RANK:, :] = -basis[...]
    basis_copy.wait_recv()
    signed_ref[0:RANK, :] = bprior[...]
    for j in range(2):
        for dx, dc in others:
            pass_copy(j, dx, dc).wait()
    for q in range(16):
        pair_ref[0:RANK, q * LANES : (q + 1) * LANES] = fprior[q]
    basis_copy.wait_send()
    for j in range(2):
        up_copy(j).wait_send()
    for i in range(PIECES):
        weight_copy(i).wait_send()
    own_copy.wait_send()
    other_copy.wait_send()
    for j in range(2):
        down_copy(j).wait_send()
        for dx, dc in others:
            spread_copy(j, dx, dc).wait_send()
            prior_copy(j, dx, dc).wait_send()


def on_device(weights, warm_factor):
    local_weight = weights[0]
    vmem = pl.BlockSpec(memory_space=pltpu.VMEM)
    dma = pltpu.SemaphoreType.DMA
    signed, factor_pair, new_factor = pl.pallas_call(
        kernel,
        out_shape=(
            jax.ShapeDtypeStruct((2 * RANK, ROWS), BF16),
            jax.ShapeDtypeStruct((2 * RANK, WID), BF16),
            jax.ShapeDtypeStruct((RANK, LANES), F32),
        ),
        in_specs=[pl.BlockSpec(memory_space=pl.ANY), vmem],
        out_specs=(vmem, vmem, vmem),
        scratch_shapes=[
            pltpu.VMEM((2 * ROWS, WID), BF16),
            pltpu.VMEM((WID, 2 * ROWS), BF16),
            pltpu.VMEM((16, RANK, LANES), BF16),
            pltpu.VMEM((16, RANK, LANES), BF16),
            pltpu.VMEM((RANK, ROWS), BF16),
            pltpu.VMEM((LANES, ROWS), F32),
            pltpu.VMEM((2 * RANK, 2 * ROWS), BF16),
            pltpu.VMEM((2, 8, RANK, LANES), F32),
            pltpu.VMEM((2, 8, RANK, LANES), F32),
            pltpu.VMEM((8, LANES), F32),
            pltpu.VMEM((8, 8, LANES), F32),
            pltpu.VMEM((2, 8, LANES), F32),
            pltpu.VMEM((2, 8, LANES), F32),
            pltpu.VMEM((2, 2, RANK, LANES), F32),
            pltpu.VMEM((2, 2, RANK, LANES), F32),
            pltpu.VMEM((LANES, LANES), F32),
            pltpu.VMEM((RANK, ROWS), BF16),
            pltpu.VMEM((16, RANK, LANES), BF16),
            pltpu.VMEM((RANK, ROWS), F32),
            pltpu.VMEM((RANK, ROWS), F32),
            pltpu.VMEM((RANK, ROWS), F32),
            pltpu.VMEM((RANK, ROWS), F32),
            pltpu.VMEM((4 * RANK, ROWS), BF16),
            pltpu.VMEM((2, 8, RANK, LANES), F32),
            pltpu.VMEM((2, 8, RANK, LANES), F32),
            pltpu.VMEM((2, RANK, LANES), F32),
            pltpu.VMEM((2, RANK, LANES), F32),
            dma((CHUNKS,)),
            dma((PIECES,)),
            dma((PIECES,)),
            dma((8,)),
            dma((8,)),
            dma((2, 8)),
            dma((2, 8)),
            dma((2, 2)),
            dma((2, 2)),
            dma((2,)),
            dma((2,)),
            dma((2, 8)),
            dma((2, 8)),
            dma((2,)),
            dma((2,)),
            dma,
            dma,
            dma((2, 8)),
            dma((2, 8)),
            dma((2,)),
            dma((2,)),
            dma((2, 8)),
            dma((2, 8)),
            dma((2,)),
            dma((2,)),
            dma((2, 8)),
            dma((2, 8)),
            dma((2,)),
            dma((2,)),
        ],
        compiler_params=pltpu.CompilerParams(
            collective_id=0, has_side_effects=True, vmem_limit_bytes=48 * 2**20
        ),
        name="power_rounds",
    )(local_weight, warm_factor[0])
    delta = jnp.einsum("jr,jc->rc", signed, factor_pair, preferred_element_type=F32)
    new_weight = (local_weight.astype(F32) + MIXING * delta).astype(BF16)
    return (new_weight[None], new_factor[None])


def solution(mesh):
    return jax.shard_map(
        on_device,
        mesh=mesh,
        in_specs=(P("blk", "shard", None), P("blk", None, None)),
        out_specs=(P("blk", "shard", None), P("blk", None, "shard")),
        check_vma=False,
    )
```
